128 devices in a mesh: row: 8 (over x, core), col: 16 (over y, z).
Axes of the slice: x: 4, y: 4, z: 4, core: 2. Of those that a mesh axis runs over, the one named last changes fastest.
Arguments:
- currents: float32 [32768, 256], P(('row', 'col')), may hold values from -6 to 6
- branch_owner: int32 [32768, 2], P(('row', 'col')), may hold values from 0 to 127, all different within a row; in each aligned block of 256 rows (0 to 255, 256 to 511, ...) at most 16 rows name the same one
- branch_slot: int32 [32768, 2], P(('row', 'col')), may hold values from 0 to 1023
- history: bfloat16 [4, 131072, 256], P(None, 'col'), may hold values from -6 to 6
- coefficients: bfloat16 [4096, 131072], P('row', 'col'), may hold values from -0.0234375 to 0.0234375
- delays: int32 [16, 512], P('row', 'col'), may hold values from 0 to 4
- slab_owner: int32 [8192, 2], P(('row', 'col')), may hold values from 0 to 127, all different within a row; in each aligned block of 64 rows (0 to 63, 64 to 127, ...) at most 4 rows name the same one
- slab_offset: int32 [8192, 2], P(('row', 'col')), may hold values from 0 to 31
Outputs:
- charge_now: bfloat16 [131072, 256], P('col')
- drops: float32 [8192, 256], P(('row', 'col'))
The draws below stay inside these ranges and needn't reach their ends.
Inputs may be any that keep to these rules, and one draw needn't show every extreme that they name: `branch_owner`: the two ends of a branch have different owners; among the rows of one device no owner is named more than 16 times. `slab_owner`: the two ends of a slab branch have different owners; among the rows of one device no owner is named more than 4 times.
All inputs are finite; a program needn't handle non-finite values.
Results may differ from the reference program's by a relative error of at most 0.0015.
Values may be sent and summed in bfloat16 or wider, within the bound.
A program may use at most 128 MiB of HBM per device.

```python
import math
import jax
import jax.numpy as jnp
import numpy as np
from jax import lax

NODES = 131072
SLAB = 4096
BLK = 256
HIST = 4
EXC = 256
BR_DEV = 256
BRANCHES = 32768
CAP = 16
OWN = 1024
SLAB_BR = 8192
SHARE = 32
SCAP = 4
DEVICES = 128


def set_ends(entries, rng, least, largest):
    shape = entries.shape
    spot = [jax.random.randint(jax.random.fold_in(rng, axis), (), 0, shape[axis]) for axis in range(len(shape))]
    entries = entries.at[tuple(spot)].set(least)
    longest = shape.index(max(shape))
    spot[longest] = (spot[longest] + 1) % shape[longest]
    return entries.at[tuple(spot)].set(largest)


def with_spikes(entries, stream_key, source, target, parts, factor):
    def block_of(position):
        return (jnp.arange(entries.shape[position]) // (entries.shape[position] // parts)).reshape((-1,) + (1,) * (entries.ndim - 1 - position))

    near = jax.random.permutation(stream_key, parts)[block_of(target)]
    far = (block_of(target) + parts // 2) % parts
    return jnp.where((block_of(source) == near) | (block_of(source) == far), factor * entries, entries)


def level_of(rng, dims, shards, smallest, high):
    factor_of = 1.0
    for axis_at, shards_of in shards:
        steps = jax.random.uniform(jax.random.fold_in(jax.random.fold_in(rng, 6), axis_at), (shards_of,), jnp.float32, smallest / len(shards), high / len(shards))
        factor_of = factor_of * jnp.repeat(jnp.exp(steps), dims[axis_at] // shards_of).reshape((-1,) + (1,) * (len(dims) - 1 - axis_at))
    return factor_of


def shared_out(stream_key, own, number, rows, count, top, reach, lean):
    sequence = jax.random.permutation(stream_key, count)
    packed, common = shares(count, rows * top, reach, lean, True), shares(count, rows * top, reach, lean, False)
    places = jnp.arange(count)

    def named(tallies, rotation):
        used = int((tallies > 0).sum())
        fixed = max(1, used // 4)
        moved = fixed + (places - fixed + rotation * (used - fixed)) % max(1, count - fixed)
        return jnp.zeros((count,), jnp.int32).at[sequence[jnp.where(places < fixed, places, moved)]].set(jnp.asarray(tallies, jnp.int32))

    tallies = jnp.where(number % 4 == 0, named(packed, number // 4), named(common, number - number // 4 - 1))
    mixed = jax.random.permutation(jax.random.fold_in(own, 3), count)
    source_of, receiver = mixed[0:count // 2 * 2:2], mixed[1:count // 2 * 2:2]
    margin = jnp.minimum(tallies[source_of] - 1, reach - tallies[receiver]) // 2
    margin = jnp.where((source_of == sequence[0]) | (receiver == sequence[0]) | (tallies[receiver] == 0), 0, jnp.maximum(margin, 0))
    moved = jax.random.randint(jax.random.fold_in(own, 4), (count // 2,), 0, 1 << 20) % (margin + 1)
    tallies = tallies.at[source_of].add(-moved).at[receiver].add(moved)
    members = jnp.searchsorted(jnp.cumsum(tallies), jnp.arange(rows * top), side="right").astype(jnp.int32)
    listing = members.reshape(top, rows).T
    listing = listing[jax.random.permutation(jax.random.fold_in(own, 1), rows)]
    rotation = jax.random.randint(jax.random.fold_in(own, 2), (rows, 1), 0, top)
    return jnp.take_along_axis(listing, (jnp.arange(top)[None, :] + rotation) % top, axis=1)


def shares(count, total, bound, slope, full):
    loads = [(1 << 20) // math.isqrt(standing ** slope) + 1 for standing in range(1, count + 1)]
    largest = bound if full else min(bound, max(-(-total // count), total * loads[0] // sum(loads)))
    least = 1 if total - largest >= count - 1 else 0
    holding, rest = [largest] + [least] * (count - 1), total - largest - least * (count - 1)
    while rest > 0:
        movable = [i for i in range(1, count) if holding[i] < largest] or [i for i in range(1, count) if holding[i] < bound]
        mass, left = sum([loads[i] for i in movable]), rest
        for i in movable:
            more = min(bound - holding[i], max(1, left * loads[i] // mass), rest)
            holding[i] = holding[i] + more
            rest = rest - more
    return np.array(holding)


def noise(own_key, dims, deviation, limit, cuts=(), kind=jnp.bfloat16):
    values = deviation * jax.random.normal(own_key, dims, jnp.float32)
    if cuts:
        values = values * level_of(own_key, dims, cuts, -0.22, 0.18)
    return jnp.clip(values, -limit, limit).astype(kind)


def noise_with(key, extent, scale, reach, split, heavy, kind=jnp.bfloat16):
    result = scale * jax.random.normal(key, extent, jnp.float32)
    if split:
        result = result * level_of(key, extent, split, -0.22, 0.18)
    return jnp.clip(with_spikes(result, jax.random.fold_in(key, 3), *heavy), -reach, reach).astype(kind)


def setup_inputs(seed: int = 0) -> dict:
    streams_of = jax.random.split(jax.random.key(seed), 9)
    currents = noise(streams_of[0], (BRANCHES, EXC), 1.0, 6.0, ((0, 128),), jnp.float32)
    branch_owner_keys = jax.random.split(jax.random.fold_in(streams_of[1], 1), BRANCHES // BR_DEV)
    branch_owner_turns = jax.random.permutation(jax.random.fold_in(streams_of[1], 3), BRANCHES // BR_DEV)
    branch_owner = jax.vmap(lambda own, number: shared_out(jax.random.fold_in(streams_of[1], 2), own, number, BR_DEV, DEVICES, 2, CAP, 2))(branch_owner_keys, branch_owner_turns).reshape((BRANCHES, 2))
    branch_slot = set_ends(jax.random.randint(streams_of[2], (BRANCHES, 2), 0, OWN), jax.random.fold_in(streams_of[2], 1), 0, OWN - 1).astype(jnp.int32)
    history = noise(streams_of[3], (HIST, NODES, EXC), 1.0, 6.0, ((1, 16),))
    coefficients = noise_with(streams_of[4], (SLAB, NODES), NODES ** -0.5, 0.0234375, ((0, 8), (1, 16)), (1, 0, 16, 2.0))
    delays = set_ends(jax.random.randint(streams_of[5], (SLAB // BLK, NODES // BLK), 0, HIST + 1), jax.random.fold_in(streams_of[5], 1), 0, HIST).astype(jnp.int32)
    slab_owner_keys = jax.random.split(jax.random.fold_in(streams_of[6], 1), SLAB_BR // (SLAB_BR // DEVICES))
    slab_owner_turns = jax.random.permutation(jax.random.fold_in(streams_of[6], 3), SLAB_BR // (SLAB_BR // DEVICES))
    slab_owner = jax.vmap(lambda own, number: shared_out(jax.random.fold_in(streams_of[6], 2), own, number, SLAB_BR // DEVICES, DEVICES, 2, SCAP, 1))(slab_owner_keys, slab_owner_turns).reshape((SLAB_BR, 2))
    slab_offset = set_ends(jax.random.randint(streams_of[7], (SLAB_BR, 2), 0, SHARE), jax.random.fold_in(streams_of[7], 1), 0, SHARE - 1).astype(jnp.int32)
    return {"currents": currents, "branch_owner": branch_owner, "branch_slot": branch_slot, "history": history, "coefficients": coefficients, "delays": delays, "slab_owner": slab_owner, "slab_offset": slab_offset}


def reference(currents, branch_owner, branch_slot, history, coefficients, delays, slab_owner, slab_offset):
    ends = branch_owner * OWN + branch_slot
    increment = jnp.zeros((NODES, EXC), jnp.float32)
    increment = increment.at[ends[:, 1]].add(currents)
    increment = increment.at[ends[:, 0]].add(-currents)
    charge_now = (history[0].astype(jnp.float32) + increment).astype(jnp.bfloat16)
    col_blocks = NODES // BLK
    now_blocks = charge_now.reshape(col_blocks, BLK, EXC)
    past_blocks = history.reshape(HIST, col_blocks, BLK, EXC)
    coef_blocks = coefficients.reshape(SLAB // BLK, BLK, NODES)
    column_ids = jnp.arange(col_blocks, dtype=jnp.int32)

    def one_block(pair):
        coef_rows, delay_row = pair
        earlier = past_blocks[jnp.maximum(delay_row - 1, 0), column_ids]
        source = jnp.where((delay_row == 0)[:, None, None], now_blocks, earlier)
        return jnp.dot(coef_rows.astype(jnp.float32), source.reshape(NODES, EXC).astype(jnp.float32), preferred_element_type=jnp.float32)

    potentials = lax.map(one_block, (coef_blocks, delays)).reshape(SLAB, EXC)
    slab_nodes = (slab_owner * SHARE + slab_offset).astype(jnp.int32)
    drops = potentials[slab_nodes[:, 0]] - potentials[slab_nodes[:, 1]]
    return charge_now, drops
```

```python
import functools

import jax
import jax.numpy as jnp
from jax import lax
from jax.experimental import pallas as pl
from jax.experimental.pallas import tpu as pltpu
from jax.sharding import PartitionSpec as P

F32 = jnp.float32
BF16 = jnp.bfloat16
I32 = jnp.int32
MESH = pl.DeviceIdType.MESH

ROWS = 8
COLS = 16
DEV = ROWS * COLS
CORES = 2
XS = ROWS // CORES
BRANCH = 256
CAP = 16
SCAP = 4
OWN = 1024
EXC = 256
HALF = 128
SLOTS = DEV * CAP
BLK = 256
PIECES = 4
PIECE = OWN // PIECES


def iota(shape, dim):
    return lax.broadcasted_iota(I32, shape, dim)


def nn(a, b):
    return lax.dot_general(a, b, (((1,), (0,)), ((), ())), preferred_element_type=F32)


def nt(a, b):
    return lax.dot_general(a, b, (((1,), (1,)), ((), ())), preferred_element_type=F32)


def tn(a, b):
    return lax.dot_general(a, b, (((0,), (0,)), ((), ())), preferred_element_type=F32)


def device_of(index):
    return (index // COLS, lax.rem(index, COLS))


def ranks_of(first, second):
    n = first.shape[1]
    hot_a = iota((DEV, n), 0) == first
    hot_b = iota((DEV, n), 0) == second
    a, b = hot_a.astype(F32), hot_b.astype(F32)
    before = (iota((n, n), 0) < iota((n, n), 1)).astype(BF16)
    seen_a = nn(a.astype(BF16), before)
    seen_b = nn(b.astype(BF16), before) + jnp.sum(a, axis=1, keepdims=True)
    rank_a = jnp.sum(a * seen_a, axis=0, keepdims=True).astype(I32)
    rank_b = jnp.sum(b * seen_b, axis=0, keepdims=True).astype(I32)
    return a.astype(BF16), b.astype(BF16), rank_a, rank_b


def greet(me):
    barrier = pltpu.get_barrier_semaphore()

    def signal(t, _):
        other = lax.rem(me + t, DEV)
        pl.semaphore_signal(barrier, inc=1, device_id=device_of(other), device_id_type=MESH)
        return 0

    lax.fori_loop(1, DEV, signal, 0)
    return barrier


def exchange_kernel(
    delays, cur, owner, slot, sowner, soffset, hist, coef,
    charge_out, acc, meta_in,
    send, recv, meta_out, planes, q_hi, q_lo, past, gathered,
    hist_a, hist_b, coef_a, coef_b,
    v_send, v_recv, m_send, m_recv, self_sem, past_sem, in_sem, out_sem,
    g_send, g_near, g_pair,
):
    row, col = lax.axis_index("row"), lax.axis_index("col")
    me = row * COLS + col
    barrier = greet(me)
    past_copy = pltpu.make_async_copy(hist.at[0, pl.ds(pl.multiple_of(row * OWN, OWN), OWN)], past, past_sem)
    past_copy.start()

    width = 2 * BLK
    steps = coef.shape[1] // width
    buffers = ((hist_a, coef_a), (hist_b, coef_b))

    def stream(step, which):
        at = pl.ds(pl.multiple_of(step * width, width), width)
        h, c = buffers[which]
        return (
            pltpu.make_async_copy(hist.at[:, at], h, in_sem.at[which, 0]),
            pltpu.make_async_copy(coef.at[:, at], c, in_sem.at[which, 1]),
        )

    for which in range(2):
        for copy in stream(which, which):
            copy.start()

    own = owner[...]
    targets = (own & (ROWS - 1)) * COLS + (own >> 3)
    t_from, t_to = targets[0:1, :], targets[1:2, :]
    hot_from, hot_to, r_from, r_to = ranks_of(t_from, t_to)
    p_from, p_to = t_from * CAP + r_from, t_to * CAP + r_to
    x = cur[...]
    size = jnp.abs(x)
    size = jnp.maximum(size[:, :HALF], size[:, HALF:])
    largest = jnp.max(size.T, axis=0, keepdims=True)
    scale = jnp.full((1, BRANCH), 2.0**-12, F32)
    inverse = jnp.full((1, BRANCH), 2.0**12, F32)
    for _ in range(32):
        smaller = largest <= scale * 16383.0
        scale = jnp.where(smaller, scale * 0.5, scale)
        inverse = jnp.where(smaller, inverse * 2.0, inverse)
    spread = jnp.broadcast_to(inverse, (HALF, BRANCH)).T
    q = jnp.round(x * jnp.concatenate([spread, spread], axis=1))
    high = jnp.floor(q * (1.0 / 256.0))
    q_hi[...] = high.astype(BF16)
    q_lo[...] = (q - high * 256.0).astype(BF16)

    def told(rank, number):
        line = iota((HALF, BRANCH), 0)
        s = number.astype(I32)
        words = jnp.where(line == rank, (s >> 5).astype(F32), 0.0)
        words = words + jnp.where(line == rank + 16, (s & 31).astype(F32), 0.0)
        return (words + jnp.where(line == rank + 32, scale, 0.0)).astype(BF16)

    s_own, s_off = sowner[...], soffset[...]
    hot_0, hot_1, s_0, s_1 = ranks_of(s_own[0:1, :], s_own[1:2, :])

    def asked(rank, offset):
        line = iota((HALF, offset.shape[1]), 0)
        return jnp.where(line == rank + 48, offset.astype(F32), 0.0).astype(BF16)

    slots = slot[...]
    words = nt(hot_from, told(r_from, slots[0:1, :])) + nt(hot_to, told(r_to, slots[1:2, :]))
    words = words + nt(hot_0, asked(s_0, s_off[0:1, :])) + nt(hot_1, asked(s_1, s_off[1:2, :]))
    meta_out[...] = words.reshape(DEV, 1, HALF)

    chunk = 256

    def fill(t, _):
        place = iota((chunk, BRANCH), 0) + t * chunk
        sign = (place == p_to).astype(F32) - (place == p_from).astype(F32)
        sign = sign.astype(BF16)
        value = (nn(sign, q_hi[...]) * 256.0 + nn(sign, q_lo[...])).astype(I32)
        word = (value[:, :HALF] << 16) | (value[:, HALF:] & 0xFFFF)
        send[pl.ds(pl.multiple_of(t * chunk, chunk), chunk), :] = word
        return 0

    lax.fori_loop(0, SLOTS // chunk, fill, 0)

    pl.semaphore_wait(barrier, DEV - 1)

    def chunk_of(index):
        return pl.ds(pl.multiple_of(index * CAP, CAP), CAP)

    def out(t, _):
        other = lax.rem(me + t, DEV)
        pltpu.make_async_remote_copy(
            meta_out.at[other], meta_in.at[me], m_send, m_recv,
            device_id=device_of(other), device_id_type=MESH,
        ).start()
        pltpu.make_async_remote_copy(
            send.at[chunk_of(other)], recv.at[chunk_of(me)], v_send, v_recv,
            device_id=device_of(other), device_id_type=MESH,
        ).start()
        return 0

    lax.fori_loop(1, DEV, out, 0)
    self_v = pltpu.make_async_copy(send.at[chunk_of(me)], recv.at[chunk_of(me)], self_sem.at[0])
    self_m = pltpu.make_async_copy(meta_out.at[me], meta_in.at[me], self_sem.at[1])
    self_v.start()
    self_m.start()

    acc[...] = jnp.zeros_like(acc)

    def delayed(pair, _):
        for which in range(2):
            step = pair * 2 + which
            for copy in stream(step, which):
                copy.wait()
            h, c = buffers[which]
            for i in range(2):
                total = acc[pl.ds(i * BLK, BLK), :]
                for k in range(2):
                    d = delays[i, step * 2 + k]
                    source = h[jnp.maximum(d - 1, 0), pl.ds(k * BLK, BLK), :]
                    part = nn(c[pl.ds(i * BLK, BLK), pl.ds(k * BLK, BLK)], source)
                    total = total + jnp.where(d > 0, part, 0.0)
                acc[pl.ds(i * BLK, BLK), :] = total

            @pl.when(pair < steps // 2 - 1)
            def _():
                for copy in stream(step + 2, which):
                    copy.start()

        return 0

    lax.fori_loop(0, steps // 2, delayed, 0)

    self_v.wait()
    self_m.wait()
    rest = pl.ds(0, DEV - 1)
    pltpu.make_async_copy(meta_in.at[rest], meta_in.at[rest], m_recv).wait()
    rest = pl.ds(0, (DEV - 1) * CAP)
    pltpu.make_async_copy(recv.at[rest], recv.at[rest], v_recv).wait()

    heard = meta_in[...].reshape(DEV, HALF).astype(BF16)
    expand = ((iota((DEV, SLOTS), 1) >> 4) == iota((DEV, SLOTS), 0)).astype(BF16)
    wide = tn(heard, expand)
    line = iota((16, SLOTS), 0)
    mine = line == (iota((16, SLOTS), 1) & 15)

    def picked(first):
        return jnp.sum(jnp.where(mine, wide[first : first + 16, :], 0.0), axis=0, keepdims=True)

    node = (picked(0) * 32.0 + picked(16)).astype(I32)
    weight = picked(32)

    def unpack(t, _):
        at = pl.ds(pl.multiple_of(t * chunk, chunk), chunk)
        w = recv[at, :]
        planes[at, 0 * HALF : 1 * HALF] = (w >> 24).astype(F32).astype(BF16)
        planes[at, 1 * HALF : 2 * HALF] = ((w << 16) >> 24).astype(F32).astype(BF16)
        planes[at, 2 * HALF : 3 * HALF] = ((w >> 16) & 255).astype(F32).astype(BF16)
        planes[at, 3 * HALF : 4 * HALF] = (w & 255).astype(F32).astype(BF16)
        return 0

    lax.fori_loop(0, SLOTS // chunk, unpack, 0)
    past_copy.wait()

    xpos, core = row // CORES, lax.rem(row, CORES)
    right, left, far = lax.rem(xpos + 1, XS), lax.rem(xpos + XS - 1, XS), lax.rem(xpos + 2, XS)

    def piece(at_x, at_core, j):
        start = (at_x * CORES + at_core) * OWN + j * PIECE
        return pl.ds(pl.multiple_of(start, PIECE), PIECE)

    def move(at_x, at_core, j, to_x, to_core, sem, recv_sem):
        at = piece(at_x, at_core, j)
        return pltpu.make_async_remote_copy(
            gathered.at[at], gathered.at[at], sem, recv_sem,
            device_id=(to_x * CORES + to_core, col), device_id_type=MESH,
        )

    sent, written = [], []

    def begin(copy):
        copy.start()
        sent.append(copy)

    def write(at_x, at_core, j, sem):
        at = piece(at_x, at_core, j)
        copy = pltpu.make_async_copy(gathered.at[at], charge_out.at[at], sem)
        copy.start()
        written.append(copy)

    order = (0, 2, 1, 3)
    other = 1 - core
    for j in order:
        spot = iota((PIECE, SLOTS), 0) + j * PIECE
        gate = jnp.where(spot == node, weight, 0.0).astype(BF16)
        both = nn(gate, planes[...])
        rise = both[:, :EXC] * 256.0 + both[:, EXC:]
        fresh = past[pl.ds(j * PIECE, PIECE), :].astype(F32) + rise
        gathered[piece(xpos, core, j), :] = fresh.astype(BF16)
        a = (right, left) if j < 2 else (left, right)
        for n, to in enumerate(a):
            side = 0 if to is right else 1
            begin(move(xpos, core, j, to, core, g_send.at[side, j], g_near.at[side, j]))
        begin(move(xpos, core, j, xpos, other, g_send.at[2, j], g_pair.at[0, j]))
        write(xpos, core, j, out_sem.at[0, j])

    def arrived(at_x, at_core, j, recv_sem):
        at = piece(at_x, at_core, j)
        pltpu.make_async_copy(gathered.at[at], gathered.at[at], recv_sem).wait()

    for j in order:
        arrived(left, core, j, g_near.at[0, j])
        if j < 2:
            begin(move(left, core, j, right, core, g_send.at[3, j], g_near.at[2, j]))
        begin(move(left, core, j, xpos, other, g_send.at[4, j], g_pair.at[1, j]))
        write(left, core, j, out_sem.at[1, j])
        arrived(right, core, j, g_near.at[1, j])
        if j >= 2:
            begin(move(right, core, j, left, core, g_send.at[3, j], g_near.at[2, j]))
        begin(move(right, core, j, xpos, other, g_send.at[5, j], g_pair.at[2, j]))
        write(right, core, j, out_sem.at[2, j])
    for j in order:
        arrived(far, core, j, g_near.at[2, j])
        begin(move(far, core, j, xpos, other, g_send.at[6, j], g_pair.at[3, j]))
        write(far, core, j, out_sem.at[3, j])
    for n, at_x in enumerate((xpos, left, right, far)):
        for j in order:
            arrived(at_x, other, j, g_pair.at[n, j])
            write(at_x, other, j, out_sem.at[4 + n, j])
    for copy in sent:
        copy.wait_send()
    for copy in written:
        copy.wait()
    rest = pl.ds(0, DEV - 1)
    pltpu.make_async_copy(meta_out.at[rest], meta_out.at[rest], m_send).wait()
    rest = pl.ds(0, (DEV - 1) * CAP)
    pltpu.make_async_copy(send.at[rest], send.at[rest], v_send).wait()


def exchange(delays, cur, owner, slot, sowner, soffset, hist, coef):
    vmem, hbm = pl.BlockSpec(memory_space=pltpu.VMEM), pl.BlockSpec(memory_space=pl.ANY)
    nodes = hist.shape[1]
    width = 2 * BLK
    dma = pltpu.SemaphoreType.DMA
    return pl.pallas_call(
        exchange_kernel,
        out_shape=(
            jax.ShapeDtypeStruct((nodes, EXC), BF16),
            jax.ShapeDtypeStruct((coef.shape[0], EXC), F32),
            jax.ShapeDtypeStruct((DEV, 1, HALF), F32),
        ),
        in_specs=[pl.BlockSpec(memory_space=pltpu.SMEM)] + [vmem] * 5 + [hbm] * 2,
        out_specs=(hbm, vmem, vmem),
        scratch_shapes=[
            pltpu.VMEM((SLOTS, HALF), I32),
            pltpu.VMEM((SLOTS, HALF), I32),
            pltpu.VMEM((DEV, 1, HALF), F32),
            pltpu.VMEM((SLOTS, 2 * EXC), BF16),
            pltpu.VMEM((BRANCH, EXC), BF16),
            pltpu.VMEM((BRANCH, EXC), BF16),
            pltpu.VMEM((OWN, EXC), BF16),
            pltpu.VMEM((nodes, EXC), BF16),
            pltpu.VMEM((4, width, EXC), BF16),
            pltpu.VMEM((4, width, EXC), BF16),
            pltpu.VMEM((coef.shape[0], width), BF16),
            pltpu.VMEM((coef.shape[0], width), BF16),
            dma, dma, dma, dma, dma((2,)), dma, dma((2, 2)), dma((8, PIECES)),
            dma((7, PIECES)), dma((3, PIECES)), dma((4, PIECES)),
        ],
        compiler_params=pltpu.CompilerParams(
            collective_id=0, has_side_effects=True, vmem_limit_bytes=48 << 20
        ),
        name="exchange",
    )(delays, cur, owner, slot, sowner, soffset, hist, coef)


def current_kernel(delays, acc, charge, coef, total, charge_now, block, weights, in_sem, out_sem, c_sem):
    span = 4 * BLK
    parts = charge.shape[0] // span

    def coefficient(i, k):
        at = pl.ds(pl.multiple_of(k * BLK, BLK), BLK)
        return pltpu.make_async_copy(
            coef.at[pl.ds(i * BLK, BLK), at], weights.at[i, k], c_sem.at[i, k]
        )

    def load(part):
        at = pl.ds(pl.multiple_of(part * span, span), span)
        return pltpu.make_async_copy(charge.at[at], block.at[at], in_sem.at[part])

    def save(part):
        at = pl.ds(pl.multiple_of(part * span, span), span)
        return pltpu.make_async_copy(block.at[at], charge_now.at[at], out_sem.at[part])

    for part in range(parts):
        load(part).start()

    def ask(k, _):
        for i in range(2):
            @pl.when(delays[i, k] == 0)
            def _():
                coefficient(i, k).start()

        return 0

    lax.fori_loop(0, parts * 4, ask, 0)
    total[...] = acc[...]
    for part in range(parts):
        load(part).wait()
        save(part).start()

        def work(n, _):
            k = part * 4 + n
            for i in range(2):
                @pl.when(delays[i, k] == 0)
                def _():
                    coefficient(i, k).wait()
                    source = block[pl.ds(pl.multiple_of(k * BLK, BLK), BLK), :]
                    total[pl.ds(i * BLK, BLK), :] += nn(weights[i, k], source)

            return 0

        lax.fori_loop(0, 4, work, 0)
    for part in range(parts):
        save(part).wait()


def current(delays, acc, charge, coef):
    vmem, hbm = pl.BlockSpec(memory_space=pltpu.VMEM), pl.BlockSpec(memory_space=pl.ANY)
    dma = pltpu.SemaphoreType.DMA
    blocks = charge.shape[0] // BLK
    return pl.pallas_call(
        current_kernel,
        out_shape=(
            jax.ShapeDtypeStruct(acc.shape, F32),
            jax.ShapeDtypeStruct(charge.shape, BF16),
        ),
        in_specs=[pl.BlockSpec(memory_space=pltpu.SMEM), vmem, hbm, hbm],
        out_specs=(vmem, hbm),
        scratch_shapes=[
            pltpu.VMEM(charge.shape, BF16),
            pltpu.VMEM((2, blocks, BLK, BLK), BF16),
            dma((blocks // 4,)), dma((blocks // 4,)), dma((2, blocks)),
        ],
        compiler_params=pltpu.CompilerParams(vmem_limit_bytes=40 << 20),
        name="current",
    )(delays, acc, charge, coef)


def split(value):
    top = value.astype(BF16)
    return top, (value - top.astype(F32)).astype(BF16)


def drops_kernel(
    part, meta, sowner, drops, parts, answer, replies,
    p_send, p_recv, a_send, a_recv, self_sem,
):
    row, col = lax.axis_index("row"), lax.axis_index("col")
    me = row * COLS + col
    barrier = greet(me)
    share = part.shape[0] // COLS
    span = 2 * SCAP
    asked = DEV * span

    heard = meta[...].reshape(DEV, HALF).astype(BF16)
    expand = ((iota((DEV, asked), 1) >> 3) == iota((DEV, asked), 0)).astype(BF16)
    wide = tn(heard, expand)[48:56, :]
    mine = iota((span, asked), 0) == (iota((span, asked), 1) & (SCAP - 1))
    place = jnp.sum(jnp.where(mine, wide, 0.0), axis=0, keepdims=True).astype(I32)
    place = place + share * ((iota((1, asked), 1) >> 2) & 1)
    take = (iota((2 * share, asked), 0) == place).astype(BF16)

    pl.semaphore_wait(barrier, DEV - 1)

    def rows_of(index):
        return pl.ds(pl.multiple_of(index * share, share), share)

    def send_part(t, _):
        other = lax.rem(col + t, COLS)
        pltpu.make_async_remote_copy(
            part.at[rows_of(other)], parts.at[rows_of(col)], p_send, p_recv,
            device_id=(row, other), device_id_type=MESH,
        ).start()
        return 0

    lax.fori_loop(1, COLS, send_part, 0)
    self_p = pltpu.make_async_copy(part.at[rows_of(col)], parts.at[rows_of(col)], self_sem.at[0])
    self_p.start()

    s_own = sowner[...]
    first, second = s_own[0:1, :], s_own[1:2, :]
    _, _, r_0, r_1 = ranks_of(first, second)
    at_0, at_1 = first * span + r_0, second * span + r_1

    self_p.wait()
    rest = pl.ds(0, (COLS - 1) * share)
    pltpu.make_async_copy(parts.at[rest], parts.at[rest], p_recv).wait()
    total = parts[pl.ds(0, share), :]
    for n in range(1, COLS):
        total = total + parts[pl.ds(n * share, share), :]
    stacked = jnp.concatenate([total[:, :HALF], total[:, HALF:]], axis=0)
    top, low = split(stacked)
    answer[...] = tn(take, top) + tn(take, low)

    def chunk_of(index):
        return pl.ds(pl.multiple_of(index * span, span), span)

    def send_answer(t, _):
        other = lax.rem(me + t, DEV)
        pltpu.make_async_remote_copy(
            answer.at[chunk_of(other)], replies.at[chunk_of(me)], a_send, a_recv,
            device_id=device_of(other), device_id_type=MESH,
        ).start()
        return 0

    lax.fori_loop(1, DEV, send_answer, 0)
    self_a = pltpu.make_async_copy(answer.at[chunk_of(me)], replies.at[chunk_of(me)], self_sem.at[1])
    self_a.start()
    self_a.wait()
    rest = pl.ds(0, (DEV - 1) * span)
    pltpu.make_async_copy(replies.at[rest], replies.at[rest], a_recv).wait()
    top, low = split(replies[...])
    both = jnp.concatenate([top, low], axis=1)
    count = first.shape[1]
    line = iota((asked, count), 0)
    for half in range(2):
        shift = half * SCAP
        gate = (line == at_0 + shift).astype(F32) - (line == at_1 + shift).astype(F32)
        found = tn(gate.astype(BF16), both)
        drops[:, half * HALF : (half + 1) * HALF] = found[:, :HALF] + found[:, HALF:]
    pltpu.make_async_copy(answer.at[rest], answer.at[rest], a_send).wait()
    rest = pl.ds(0, (COLS - 1) * share)
    pltpu.make_async_copy(part.at[rest], part.at[rest], p_send).wait()


def find_drops(part, meta, sowner):
    vmem = pl.BlockSpec(memory_space=pltpu.VMEM)
    dma = pltpu.SemaphoreType.DMA
    asked = DEV * 2 * SCAP
    return pl.pallas_call(
        drops_kernel,
        out_shape=jax.ShapeDtypeStruct((sowner.shape[1], EXC), F32),
        in_specs=[vmem] * 3,
        out_specs=vmem,
        scratch_shapes=[
            pltpu.VMEM(part.shape, F32),
            pltpu.VMEM((asked, HALF), F32),
            pltpu.VMEM((asked, HALF), F32),
            dma, dma, dma, dma, dma((2,)),
        ],
        compiler_params=pltpu.CompilerParams(
            collective_id=1, has_side_effects=True, vmem_limit_bytes=24 << 20
        ),
        name="find_drops",
    )(part, meta, sowner)


def local(
    currents, branch_owner, branch_slot, history, coefficients, delays, slab_owner, slab_offset
):
    sowner = slab_owner.T
    charge, acc, meta = exchange(
        delays, currents, branch_owner.T, branch_slot.T, sowner, slab_offset.T, history, coefficients
    )
    part, charge_now = current(delays, acc, charge, coefficients)
    return charge_now, find_drops(part, meta, sowner)


def solution(mesh):
    placed = (
        P(("row", "col"), None),
        P(("row", "col"), None),
        P(("row", "col"), None),
        P(None, "col", None),
        P("row", "col"),
        P("row", "col"),
        P(("row", "col"), None),
        P(("row", "col"), None),
    )
    return jax.shard_map(
        local,
        mesh=mesh,
        in_specs=placed,
        out_specs=(P("col", None), P(("row", "col"), None)),
        check_vma=False,
    )
```

```python
import functools

import jax
import jax.numpy as jnp
from jax import lax
from jax.experimental import pallas as pl
from jax.experimental.pallas import tpu as pltpu
from jax.sharding import PartitionSpec as P

F32 = jnp.float32
BF16 = jnp.bfloat16
I32 = jnp.int32
MESH = pl.DeviceIdType.MESH

ROWS = 8
COLS = 16
DEV = ROWS * COLS
CORES = 2
XS = ROWS // CORES
BRANCH = 256
CAP = 16
SCAP = 4
OWN = 1024
EXC = 256
HALF = 128
SLOTS = DEV * CAP
BLK = 256
PIECES = 4
PIECE = OWN // PIECES


def iota(shape, dim):
    return lax.broadcasted_iota(I32, shape, dim)


def nn(a, b):
    return lax.dot_general(a, b, (((1,), (0,)), ((), ())), preferred_element_type=F32)


def nt(a, b):
    return lax.dot_general(a, b, (((1,), (1,)), ((), ())), preferred_element_type=F32)


def tn(a, b):
    return lax.dot_general(a, b, (((0,), (0,)), ((), ())), preferred_element_type=F32)


def device_of(index):
    return (index // COLS, lax.rem(index, COLS))


def ranks_of(first, second):
    n = first.shape[1]
    hot_a = iota((DEV, n), 0) == first
    hot_b = iota((DEV, n), 0) == second
    a, b = hot_a.astype(F32), hot_b.astype(F32)
    before = (iota((n, n), 0) < iota((n, n), 1)).astype(BF16)
    seen_a = nn(a.astype(BF16), before)
    seen_b = nn(b.astype(BF16), before) + jnp.sum(a, axis=1, keepdims=True)
    rank_a = jnp.sum(a * seen_a, axis=0, keepdims=True).astype(I32)
    rank_b = jnp.sum(b * seen_b, axis=0, keepdims=True).astype(I32)
    return a.astype(BF16), b.astype(BF16), rank_a, rank_b


def greet(me):
    barrier = pltpu.get_barrier_semaphore()

    def signal(t, _):
        other = lax.rem(me + t, DEV)
        pl.semaphore_signal(barrier, inc=1, device_id=device_of(other), device_id_type=MESH)
        return 0

    lax.fori_loop(1, DEV, signal, 0)
    return barrier


def step_kernel(
    cur_h, owner_h, slot_h, sowner_h, soffset_h, hist, coef_h, delays_h,
    gathered, drops,
    cur, owner, slot, sowner, soffset, delays,
    send, recv, meta_out, meta_in, planes, q_hi, q_lo, past, coef, hist_a, hist_b, acc,
    take, gates, p_send, p_recv, ps_send, ps_recv, answer, replies, as_send, as_recv,
    first_sem, v_send, v_recv, m_send, m_recv, self_sem, past_sem, h_sem, c_sem,
    g_send, g_near, g_pair, r_send, r_recv, rs_send, rs_recv, a_send, a_recv, b_send, b_recv,
):
    row, col = lax.axis_index("row"), lax.axis_index("col")
    me = row * COLS + col
    barrier = greet(me)
    small = ((cur_h, cur), (owner_h, owner), (slot_h, slot), (sowner_h, sowner), (soffset_h, soffset), (delays_h, delays))
    small = [pltpu.make_async_copy(a, b, first_sem.at[n]) for n, (a, b) in enumerate(small)]
    for copy in small:
        copy.start()
    past_copy = pltpu.make_async_copy(hist.at[0, pl.ds(pl.multiple_of(row * OWN, OWN), OWN)], past, past_sem)
    past_copy.start()

    width = 2 * BLK
    steps = coef.shape[0]
    buffers = (hist_a, hist_b)

    def stream(step, which):
        at = pl.ds(pl.multiple_of(step * width, width), width)
        return (
            pltpu.make_async_copy(hist.at[:, at], buffers[which], h_sem.at[which]),
            pltpu.make_async_copy(coef_h.at[:, at], coef.at[step], c_sem.at[which]),
        )

    for which in range(2):
        for copy in stream(which, which):
            copy.start()
    for copy in small:
        copy.wait()

    own = owner[...]
    targets = (own & (ROWS - 1)) * COLS + (own >> 3)
    t_from, t_to = targets[0:1, :], targets[1:2, :]
    hot_from, hot_to, r_from, r_to = ranks_of(t_from, t_to)
    p_from, p_to = t_from * CAP + r_from, t_to * CAP + r_to
    x = cur[...]
    size = jnp.abs(x)
    size = jnp.maximum(size[:, :HALF], size[:, HALF:])
    largest = jnp.max(size.T, axis=0, keepdims=True)
    scale = jnp.full((1, BRANCH), 2.0**-12, F32)
    inverse = jnp.full((1, BRANCH), 2.0**12, F32)
    for _ in range(32):
        smaller = largest <= scale * 16383.0
        scale = jnp.where(smaller, scale * 0.5, scale)
        inverse = jnp.where(smaller, inverse * 2.0, inverse)
    spread = jnp.broadcast_to(inverse, (HALF, BRANCH)).T
    q = jnp.round(x * jnp.concatenate([spread, spread], axis=1))
    high = jnp.floor(q * (1.0 / 256.0))
    q_hi[...] = high.astype(BF16)
    q_lo[...] = (q - high * 256.0).astype(BF16)

    def told(rank, number):
        line = iota((HALF, BRANCH), 0)
        words = jnp.where(line == rank, (number >> 5).astype(F32), 0.0)
        words = words + jnp.where(line == rank + 16, (number & 31).astype(F32), 0.0)
        return (words + jnp.where(line == rank + 32, scale, 0.0)).astype(BF16)

    s_own, s_off = sowner[...], soffset[...]
    s_from, s_to = s_own[0:1, :], s_own[1:2, :]
    hot_0, hot_1, s_0, s_1 = ranks_of(s_from, s_to)

    def asked(rank, offset):
        line = iota((HALF, offset.shape[1]), 0)
        return jnp.where(line == rank + 48, offset.astype(F32), 0.0).astype(BF16)

    slots = slot[...]
    words = nt(hot_from, told(r_from, slots[0:1, :])) + nt(hot_to, told(r_to, slots[1:2, :]))
    words = words + nt(hot_0, asked(s_0, s_off[0:1, :])) + nt(hot_1, asked(s_1, s_off[1:2, :]))
    meta_out[...] = words.reshape(DEV, 1, HALF)

    chunk = 256

    def word_of(value):
        return (value[:, :HALF] << 16) | (value[:, HALF:] & 0xFFFF)

    def fill(t, _):
        place = iota((chunk, BRANCH), 0) + t * chunk
        sign = (place == p_to).astype(F32) - (place == p_from).astype(F32)
        sign = sign.astype(BF16)
        value = (nn(sign, q_hi[...]) * 256.0 + nn(sign, q_lo[...])).astype(I32)
        send[pl.ds(pl.multiple_of(t * chunk, chunk), chunk), :] = word_of(value)
        return 0

    lax.fori_loop(0, SLOTS // chunk, fill, 0)

    pl.semaphore_wait(barrier, DEV - 1)

    def chunk_of(index):
        return pl.ds(pl.multiple_of(index * CAP, CAP), CAP)

    def out(t, _):
        other = lax.rem(me + t, DEV)
        pltpu.make_async_remote_copy(
            meta_out.at[other], meta_in.at[me], m_send, m_recv,
            device_id=device_of(other), device_id_type=MESH,
        ).start()
        pltpu.make_async_remote_copy(
            send.at[chunk_of(other)], recv.at[chunk_of(me)], v_send, v_recv,
            device_id=device_of(other), device_id_type=MESH,
        ).start()
        return 0

    lax.fori_loop(1, DEV, out, 0)
    self_v = pltpu.make_async_copy(send.at[chunk_of(me)], recv.at[chunk_of(me)], self_sem.at[0])
    self_m = pltpu.make_async_copy(meta_out.at[me], meta_in.at[me], self_sem.at[1])
    self_v.start()
    self_m.start()

    span = 2 * SCAP
    asks = DEV * span
    line = iota((asks, s_own.shape[1]), 0)
    gate = (line == s_from * span + s_0).astype(F32) - (line == s_to * span + s_1).astype(F32)
    gates[...] = gate.astype(BF16)

    acc[...] = jnp.zeros_like(acc)

    def delayed(pair, _):
        for which in range(2):
            step = pair * 2 + which
            for copy in stream(step, which):
                copy.wait()
            h = buffers[which]
            for i in range(2):
                total = acc[pl.ds(i * BLK, BLK), :]
                for k in range(2):
                    d = delays[i, step * 2 + k]
                    source = h[jnp.maximum(d - 1, 0), pl.ds(k * BLK, BLK), :]
                    part = nn(coef[step, pl.ds(i * BLK, BLK), pl.ds(k * BLK, BLK)], source)
                    total = total + jnp.where(d > 0, part, 0.0)
                acc[pl.ds(i * BLK, BLK), :] = total

            @pl.when(pair < steps // 2 - 1)
            def _():
                for copy in stream(step + 2, which):
                    copy.start()

        return 0

    lax.fori_loop(0, steps // 2, delayed, 0)

    self_m.wait()
    rest = pl.ds(0, DEV - 1)
    pltpu.make_async_copy(meta_in.at[rest], meta_in.at[rest], m_recv).wait()
    heard = meta_in[...].reshape(DEV, HALF).astype(BF16)
    expand = ((iota((DEV, SLOTS), 1) >> 4) == iota((DEV, SLOTS), 0)).astype(BF16)
    wide = tn(heard, expand)
    line = iota((16, SLOTS), 0)
    mine = line == (iota((16, SLOTS), 1) & 15)

    def picked(first):
        return jnp.sum(jnp.where(mine, wide[first : first + 16, :], 0.0), axis=0, keepdims=True)

    node = (picked(0) * 32.0 + picked(16)).astype(I32)
    weight = picked(32)

    share = acc.shape[0] // COLS
    expand = ((iota((DEV, asks), 1) >> 3) == iota((DEV, asks), 0)).astype(BF16)
    wide = tn(heard, expand)[48:56, :]
    line = iota((span, asks), 0)
    mine = line == (iota((span, asks), 1) & (span - 1))
    place = jnp.sum(jnp.where(mine, wide, 0.0), axis=0, keepdims=True).astype(I32)
    take[...] = (iota((share, asks), 0) == place).astype(BF16)

    self_v.wait()
    rest = pl.ds(0, (DEV - 1) * CAP)
    pltpu.make_async_copy(recv.at[rest], recv.at[rest], v_recv).wait()

    def unpack(t, _):
        at = pl.ds(pl.multiple_of(t * chunk, chunk), chunk)
        w = recv[at, :]
        planes[at, 0 * HALF : 1 * HALF] = (w >> 24).astype(F32).astype(BF16)
        planes[at, 1 * HALF : 2 * HALF] = ((w << 16) >> 24).astype(F32).astype(BF16)
        planes[at, 2 * HALF : 3 * HALF] = ((w >> 16) & 255).astype(F32).astype(BF16)
        planes[at, 3 * HALF : 4 * HALF] = (w & 255).astype(F32).astype(BF16)
        return 0

    lax.fori_loop(0, SLOTS // chunk, unpack, 0)
    past_copy.wait()

    xpos, core = row // CORES, lax.rem(row, CORES)
    right, left, far = lax.rem(xpos + 1, XS), lax.rem(xpos + XS - 1, XS), lax.rem(xpos + 2, XS)
    other = 1 - core

    def piece(at_x, at_core, j):
        start = (at_x * CORES + at_core) * OWN + j * PIECE
        return pl.ds(pl.multiple_of(start, PIECE), PIECE)

    def move(at_x, at_core, j, to_x, to_core, sem, recv_sem):
        at = piece(at_x, at_core, j)
        return pltpu.make_async_remote_copy(
            gathered.at[at], gathered.at[at], sem, recv_sem,
            device_id=(to_x * CORES + to_core, col), device_id_type=MESH,
        )

    def arrived(at_x, at_core, j, recv_sem):
        at = piece(at_x, at_core, j)
        pltpu.make_async_copy(gathered.at[at], gathered.at[at], recv_sem).wait()

    def use(at_x, at_core, j):
        block = (at_x * CORES + at_core) * PIECES + j
        source = gathered[piece(at_x, at_core, j), :]
        at = pl.ds(pl.multiple_of(lax.rem(j, 2) * BLK, BLK), BLK)
        for i in range(2):
            part = nn(coef[block // 2, pl.ds(i * BLK, BLK), at], source)
            acc[pl.ds(i * BLK, BLK), :] += jnp.where(delays[i, block] == 0, part, 0.0)

    def turn(t):
        return lax.rem(t, 2) * 2 + t // 2

    def settle(t, _):
        j = turn(t)
        spot = iota((PIECE, SLOTS), 0) + j * PIECE
        gate = jnp.where(spot == node, weight, 0.0).astype(BF16)
        both = nn(gate, planes[...])
        rise = both[:, :EXC] * 256.0 + both[:, EXC:]
        fresh = past[pl.ds(pl.multiple_of(j * PIECE, PIECE), PIECE), :].astype(F32) + rise
        gathered[piece(xpos, core, j), :] = fresh.astype(BF16)
        move(xpos, core, j, right, core, g_send.at[0, j], g_near.at[0, j]).start()
        move(xpos, core, j, left, core, g_send.at[1, j], g_near.at[1, j]).start()
        move(xpos, core, j, xpos, other, g_send.at[2, j], g_pair.at[0, j]).start()
        return 0

    lax.fori_loop(0, PIECES, settle, 0)

    def near(t, _):
        j = turn(t)
        arrived(left, core, j, g_near.at[0, j])

        @pl.when(j < 2)
        def _():
            move(left, core, j, right, core, g_send.at[3, j], g_near.at[2, j]).start()

        move(left, core, j, xpos, other, g_send.at[4, j], g_pair.at[1, j]).start()
        use(xpos, core, j)
        arrived(right, core, j, g_near.at[1, j])

        @pl.when(j >= 2)
        def _():
            move(right, core, j, left, core, g_send.at[3, j], g_near.at[2, j]).start()

        move(right, core, j, xpos, other, g_send.at[5, j], g_pair.at[2, j]).start()
        use(left, core, j)
        use(right, core, j)
        arrived(xpos, other, j, g_pair.at[0, j])
        use(xpos, other, j)
        return 0

    lax.fori_loop(0, PIECES, near, 0)

    def distant(t, _):
        j = turn(t)
        arrived(far, core, j, g_near.at[2, j])
        move(far, core, j, xpos, other, g_send.at[6, j], g_pair.at[3, j]).start()
        arrived(left, other, j, g_pair.at[1, j])
        use(left, other, j)
        arrived(right, other, j, g_pair.at[2, j])
        use(right, other, j)
        use(far, core, j)
        return 0

    lax.fori_loop(0, PIECES, distant, 0)

    def last(t, _):
        j = turn(t)
        arrived(far, other, j, g_pair.at[3, j])
        use(far, other, j)
        return 0

    lax.fori_loop(0, PIECES, last, 0)

    def rows_of(index):
        return pl.ds(pl.multiple_of(index * share, share), share)

    def coded(value, top):
        number = jnp.round(value * (32767.0 / jnp.maximum(top, 1e-30)))
        return number

    def give(t, _):
        to = lax.rem(col + t, COLS)
        value = acc[rows_of(to), :]
        top = jnp.max(jnp.abs(value), axis=0, keepdims=True)
        p_send[rows_of(to), :] = word_of(coded(value, top).astype(I32))
        ps_send[to, 0:1, :] = top[:, :HALF]
        ps_send[to, 1:2, :] = top[:, HALF:]

        @pl.when(t < COLS)
        def _():
            pltpu.make_async_remote_copy(
                ps_send.at[to], ps_recv.at[col], rs_send, rs_recv,
                device_id=(row, to), device_id_type=MESH,
            ).start()
            pltpu.make_async_remote_copy(
                p_send.at[rows_of(to)], p_recv.at[rows_of(col)], r_send, r_recv,
                device_id=(row, to), device_id_type=MESH,
            ).start()

        return 0

    lax.fori_loop(1, COLS + 1, give, 0)
    self_p = pltpu.make_async_copy(p_send.at[rows_of(col)], p_recv.at[rows_of(col)], self_sem.at[2])
    self_s = pltpu.make_async_copy(ps_send.at[col], ps_recv.at[col], self_sem.at[3])
    self_p.start()
    self_s.start()
    self_p.wait()
    self_s.wait()
    rest = pl.ds(0, COLS - 1)
    pltpu.make_async_copy(ps_recv.at[rest], ps_recv.at[rest], rs_recv).wait()
    rest = pl.ds(0, (COLS - 1) * share)
    pltpu.make_async_copy(p_recv.at[rest], p_recv.at[rest], r_recv).wait()

    def gain(n, totals):
        w = p_recv[rows_of(n), :]
        top = ps_recv[n] * (1.0 / 32767.0)
        a = totals[0] + (w >> 16).astype(F32) * top[0:1, :]
        b = totals[1] + ((w << 16) >> 16).astype(F32) * top[1:2, :]
        return a, b

    zero = jnp.zeros((share, HALF), F32)
    a, b = lax.fori_loop(0, COLS, gain, (zero, zero))

    top = jnp.max(jnp.maximum(jnp.abs(a), jnp.abs(b)), axis=0, keepdims=True)
    as_send[...] = top.reshape(1, 1, HALF)
    number = jnp.concatenate([coded(a, top), coded(b, top)], axis=1)
    high = jnp.floor(number * (1.0 / 256.0))
    low = (number - high * 256.0).astype(BF16)
    high = high.astype(BF16)
    for g in range(asks // HALF):
        chosen = take[:, g * HALF : (g + 1) * HALF]
        value = (tn(chosen, high) * 256.0 + tn(chosen, low)).astype(I32)
        word = word_of(value).reshape(HALF // span, span, HALF)
        answer[pl.ds(g * (HALF // span), HALF // span)] = word[:, :SCAP, :]

    def send_answer(t, _):
        to = lax.rem(me + t, DEV)
        pltpu.make_async_remote_copy(
            as_send.at[0], as_recv.at[me], b_send, b_recv,
            device_id=device_of(to), device_id_type=MESH,
        ).start()
        pltpu.make_async_remote_copy(
            answer.at[to], replies.at[me], a_send, a_recv,
            device_id=device_of(to), device_id_type=MESH,
        ).start()
        return 0

    lax.fori_loop(1, DEV, send_answer, 0)
    self_a = pltpu.make_async_copy(answer.at[me], replies.at[me], self_sem.at[4])
    self_b = pltpu.make_async_copy(as_send.at[0], as_recv.at[me], self_sem.at[5])
    self_a.start()
    self_b.start()

    for n in range(7):
        def left_here(j, _):
            at = piece(xpos, core, j)
            pltpu.make_async_copy(gathered.at[at], gathered.at[at], g_send.at[n, j]).wait()
            return 0

        lax.fori_loop(0, PIECES, left_here, 0)
    rest = pl.ds(0, DEV - 1)
    pltpu.make_async_copy(meta_out.at[rest], meta_out.at[rest], m_send).wait()
    rest = pl.ds(0, (DEV - 1) * CAP)
    pltpu.make_async_copy(send.at[rest], send.at[rest], v_send).wait()
    rest = pl.ds(0, COLS - 1)
    pltpu.make_async_copy(ps_send.at[rest], ps_send.at[rest], rs_send).wait()
    rest = pl.ds(0, (COLS - 1) * share)
    pltpu.make_async_copy(p_send.at[rest], p_send.at[rest], r_send).wait()

    self_a.wait()
    self_b.wait()
    rest = pl.ds(0, DEV - 1)
    pltpu.make_async_copy(as_recv.at[rest], as_recv.at[rest], b_recv).wait()
    pltpu.make_async_copy(replies.at[rest], replies.at[rest], a_recv).wait()
    w = replies[...]
    top = as_recv[...] * (1.0 / 32767.0)
    picks = gates[...]
    for half in range(2):
        number = (w >> 16) if half == 0 else ((w << 16) >> 16)
        value = number.astype(F32) * top
        value = jnp.concatenate([value, value], axis=1).reshape(asks, HALF)
        high, low = split(value)
        drops[:, half * HALF : (half + 1) * HALF] = tn(picks, high) + tn(picks, low)
    pltpu.make_async_copy(as_recv.at[rest], as_recv.at[rest], b_send).wait()
    pltpu.make_async_copy(answer.at[rest], answer.at[rest], a_send).wait()


def split(value):
    top = value.astype(BF16)
    return top, (value - top.astype(F32)).astype(BF16)


def step(cur, owner, slot, sowner, soffset, hist, coef, delays):
    vmem, hbm = pl.BlockSpec(memory_space=pltpu.VMEM), pl.BlockSpec(memory_space=pltpu.HBM)
    nodes, rows = hist.shape[1], coef.shape[0]
    width = 2 * BLK
    dma = pltpu.SemaphoreType.DMA
    asks = DEV * 2 * SCAP
    return pl.pallas_call(
        step_kernel,
        out_shape=(
            jax.ShapeDtypeStruct((nodes, EXC), BF16),
            jax.ShapeDtypeStruct((sowner.shape[1], EXC), F32),
        ),
        in_specs=[hbm] * 8,
        out_specs=(vmem, vmem),
        scratch_shapes=[
            pltpu.VMEM(cur.shape, F32),
            pltpu.VMEM(owner.shape, I32),
            pltpu.VMEM(slot.shape, I32),
            pltpu.VMEM(sowner.shape, I32),
            pltpu.VMEM(soffset.shape, I32),
            pltpu.SMEM(delays.shape, I32),
            pltpu.VMEM((SLOTS, HALF), I32),
            pltpu.VMEM((SLOTS, HALF), I32),
            pltpu.VMEM((DEV, 1, HALF), F32),
            pltpu.VMEM((DEV, 1, HALF), F32),
            pltpu.VMEM((SLOTS, 2 * EXC), BF16),
            pltpu.VMEM((BRANCH, EXC), BF16),
            pltpu.VMEM((BRANCH, EXC), BF16),
            pltpu.VMEM((OWN, EXC), BF16),
            pltpu.VMEM((nodes // width, rows, width), BF16),
            pltpu.VMEM((4, width, EXC), BF16),
            pltpu.VMEM((4, width, EXC), BF16),
            pltpu.VMEM((rows, EXC), F32),
            pltpu.VMEM((rows // COLS, asks), BF16),
            pltpu.VMEM((asks, sowner.shape[1]), BF16),
            pltpu.VMEM((rows, HALF), I32),
            pltpu.VMEM((rows, HALF), I32),
            pltpu.VMEM((COLS, 2, HALF), F32),
            pltpu.VMEM((COLS, 2, HALF), F32),
            pltpu.VMEM((DEV, SCAP, HALF), I32),
            pltpu.VMEM((DEV, SCAP, HALF), I32),
            pltpu.VMEM((1, 1, HALF), F32),
            pltpu.VMEM((DEV, 1, HALF), F32),
            dma((6,)), dma, dma, dma, dma, dma((6,)), dma, dma((2,)), dma((2,)),
            dma((7, PIECES)), dma((3, PIECES)), dma((4, PIECES)),
            dma, dma, dma, dma, dma, dma, dma, dma,
        ],
        compiler_params=pltpu.CompilerParams(
            collective_id=0, has_side_effects=True, vmem_limit_bytes=52 << 20
        ),
        name="step",
    )(cur, owner, slot, sowner, soffset, hist, coef, delays)


def local(
    currents, branch_owner, branch_slot, history, coefficients, delays, slab_owner, slab_offset
):
    return step(
        currents, branch_owner.T, branch_slot.T, slab_owner.T, slab_offset.T, history, coefficients, delays
    )


def solution(mesh):
    placed = (
        P(("row", "col"), None),
        P(("row", "col"), None),
        P(("row", "col"), None),
        P(None, "col", None),
        P("row", "col"),
        P("row", "col"),
        P(("row", "col"), None),
        P(("row", "col"), None),
    )
    return jax.shard_map(
        local,
        mesh=mesh,
        in_specs=placed,
        out_specs=(P("col", None), P(("row", "col"), None)),
        check_vma=False,
    )
```

```python
import functools

import jax
import jax.numpy as jnp
from jax import lax
from jax.experimental import pallas as pl
from jax.experimental.pallas import tpu as pltpu
from jax.sharding import PartitionSpec as P

F32 = jnp.float32
BF16 = jnp.bfloat16
I32 = jnp.int32
MESH = pl.DeviceIdType.MESH

ROWS = 8
COLS = 16
DEV = ROWS * COLS
CORES = 2
XS = ROWS // CORES
BRANCH = 256
CAP = 16
SCAP = 4
OWN = 1024
EXC = 256
HALF = 128
SLOTS = DEV * CAP
BLK = 256
PIECES = 4
PIECE = OWN // PIECES
FULL = 67043328
STRIDE = 1
LEAST = 2.0**-80


def iota(shape, dim):
    return lax.broadcasted_iota(I32, shape, dim)


def nn(a, b):
    return lax.dot_general(a, b, (((1,), (0,)), ((), ())), preferred_element_type=F32)


def nt(a, b):
    return lax.dot_general(a, b, (((1,), (1,)), ((), ())), preferred_element_type=F32)


def tn(a, b):
    return lax.dot_general(a, b, (((0,), (0,)), ((), ())), preferred_element_type=F32)


def power(exponent, sign):
    result = jnp.ones(exponent.shape, F32)
    for bit in range(7):
        factor = 2.0 ** (sign * (1 << bit))
        result = result * jnp.where(((exponent >> bit) & 1) > 0, factor, 1.0)
    return result


def coded(value, top):
    up = jnp.zeros(top.shape, I32)
    unit = jnp.full(top.shape, LEAST, F32)
    inverse = jnp.full(top.shape, 1.0 / LEAST, F32)
    for bit in (6, 5, 4, 3, 2, 1, 0):
        leap = 1 << bit
        larger = top > unit * (32766.0 * 2.0 ** (leap - 1))
        up = jnp.where(larger, up + leap, up)
        unit = jnp.where(larger, unit * 2.0**leap, unit)
        inverse = jnp.where(larger, inverse * 2.0**-leap, inverse)
    return up, jnp.round(value * inverse)


def device_of(index):
    return (index // COLS, lax.rem(index, COLS))


def ranks_of(first, second):
    n = first.shape[1]
    hot_a = iota((DEV, n), 0) == first
    hot_b = iota((DEV, n), 0) == second
    a, b = hot_a.astype(F32), hot_b.astype(F32)
    before = (iota((n, n), 0) < iota((n, n), 1)).astype(BF16)
    seen_a = nn(a.astype(BF16), before)
    seen_b = nn(b.astype(BF16), before) + jnp.sum(a, axis=1, keepdims=True)
    rank_a = jnp.sum(a * seen_a, axis=0, keepdims=True).astype(I32)
    rank_b = jnp.sum(b * seen_b, axis=0, keepdims=True).astype(I32)
    return a.astype(BF16), b.astype(BF16), rank_a, rank_b


def greet(me):
    barrier = pltpu.get_barrier_semaphore()

    def signal(t, _):
        other = lax.rem(me + t, DEV)
        pl.semaphore_signal(barrier, inc=1, device_id=device_of(other), device_id_type=MESH)
        return 0

    lax.fori_loop(1, DEV, signal, 0)
    return barrier


def step_kernel(
    cur_h, owner_h, slot_h, sowner_h, soffset_h, hist, coef_h, delays_h,
    charge_out, replies,
    cur, owner, slot, sowner, soffset, delays,
    send, recv, planes, q_hi, q_lo, past, coef, held, acc, gathered,
    take, p_send, p_recv, answer,
    first_sem, v_send, v_recv, self_sem, past_sem, h_sem, c_sem, w_sem,
    g_send, g_near, g_pair, r_send, r_recv, a_send, a_recv,
):
    row, col = lax.axis_index("row"), lax.axis_index("col")
    me = row * COLS + col
    barrier = greet(me)
    small = ((cur_h, cur), (owner_h, owner), (slot_h, slot), (sowner_h, sowner), (soffset_h, soffset), (delays_h, delays))
    small = [pltpu.make_async_copy(a, b, first_sem.at[n]) for n, (a, b) in enumerate(small)]
    for copy in small:
        copy.start()
    past_copy = pltpu.make_async_copy(hist.at[0, pl.ds(pl.multiple_of(row * OWN, OWN), OWN)], past, past_sem)
    past_copy.start()

    width = 2 * BLK
    steps = coef.shape[0]

    def fetch(step):
        at = pl.ds(pl.multiple_of(step * width, width), width)
        return (
            pltpu.make_async_copy(hist.at[:, at], held.at[:, at], h_sem),
            pltpu.make_async_copy(coef_h.at[:, at], coef.at[step], c_sem.at[step]),
        )

    def bring(step, _):
        for copy in fetch(step):
            copy.start()
        return 0

    lax.fori_loop(0, steps, bring, 0)
    for copy in small:
        copy.wait()

    own = owner[...]
    targets = (own & (ROWS - 1)) * COLS + (own >> 3)
    t_from, t_to = targets[0:1, :], targets[1:2, :]
    hot_from, hot_to, r_from, r_to = ranks_of(t_from, t_to)
    p_from, p_to = t_from * CAP + r_from, t_to * CAP + r_to
    x = cur[...]
    size = jnp.abs(x)
    size = jnp.maximum(size[:, :HALF], size[:, HALF:])
    largest = jnp.max(size.T, axis=0, keepdims=True)
    scale = jnp.full((1, BRANCH), 2.0**-12, F32)
    inverse = jnp.full((1, BRANCH), 2.0**12, F32)
    exponent = jnp.ones((1, BRANCH), F32)
    for _ in range(32):
        smaller = largest <= scale * 16383.0
        scale = jnp.where(smaller, scale * 0.5, scale)
        inverse = jnp.where(smaller, inverse * 2.0, inverse)
        exponent = jnp.where(smaller, exponent + 1.0, exponent)
    spread = jnp.broadcast_to(inverse, (HALF, BRANCH)).T
    q = jnp.round(x * jnp.concatenate([spread, spread], axis=1))
    high = jnp.floor(q * (1.0 / 256.0))
    q_hi[...] = high.astype(BF16)
    q_lo[...] = (q - high * 256.0).astype(BF16)

    def told(rank, number):
        line = iota((HALF, BRANCH), 0)
        words = jnp.where(line == rank, (number >> 5).astype(F32), 0.0)
        words = words + jnp.where(line == rank + 16, (number & 31).astype(F32), 0.0)
        return (words + jnp.where(line == rank + 32, exponent, 0.0)).astype(BF16)

    s_own, s_off = sowner[...], soffset[...]
    s_from, s_to = s_own[0:1, :], s_own[1:2, :]
    hot_0, hot_1, s_0, s_1 = ranks_of(s_from, s_to)

    def asked(rank, offset):
        line = iota((HALF, offset.shape[1]), 0)
        return jnp.where(line == rank + 48, offset.astype(F32), 0.0).astype(BF16)

    slots = slot[...]
    words = nt(hot_from, told(r_from, slots[0:1, :])) + nt(hot_to, told(r_to, slots[1:2, :]))
    words = words + nt(hot_0, asked(s_0, s_off[0:1, :])) + nt(hot_1, asked(s_1, s_off[1:2, :]))
    send[:, CAP : CAP + 1, :] = words.astype(I32).reshape(DEV, 1, HALF)

    chunk = 256

    def word_of(value):
        return (value[:, :HALF] << 16) | (value[:, HALF:] & 0xFFFF)

    def fill(t, _):
        place = iota((chunk, BRANCH), 0) + t * chunk
        sign = (place == p_to).astype(F32) - (place == p_from).astype(F32)
        sign = sign.astype(BF16)
        value = (nn(sign, q_hi[...]) * 256.0 + nn(sign, q_lo[...])).astype(I32)
        word = word_of(value).reshape(chunk // CAP, CAP, HALF)
        send[pl.ds(t * (chunk // CAP), chunk // CAP), 0:CAP, :] = word
        return 0

    lax.fori_loop(0, SLOTS // chunk, fill, 0)

    pl.semaphore_wait(barrier, DEV - 1)

    def out(t, _):
        other = lax.rem(me + t * STRIDE, DEV)
        pltpu.make_async_remote_copy(
            send.at[other], recv.at[me], v_send, v_recv,
            device_id=device_of(other), device_id_type=MESH,
        ).start()
        return 0

    lax.fori_loop(1, DEV, out, 0)
    self_v = pltpu.make_async_copy(send.at[me], recv.at[me], self_sem.at[0])
    self_v.start()
    span = 2 * SCAP
    asks = DEV * span

    acc[...] = jnp.zeros_like(acc)

    def landed(step, _):
        for copy in fetch(step):
            copy.wait()
        return 0

    lax.fori_loop(0, steps, landed, 0)

    def delayed(step, _):
        for i in range(2):
            total = acc[pl.ds(i * BLK, BLK), :]
            for k in range(2):
                d = delays[i, step * 2 + k]
                at = pl.ds(pl.multiple_of(step * width + k * BLK, BLK), BLK)
                source = held[jnp.maximum(d - 1, 0), at, :]
                part = nn(coef[step, pl.ds(i * BLK, BLK), pl.ds(k * BLK, BLK)], source)
                total = total + jnp.where(d > 0, part, 0.0)
            acc[pl.ds(i * BLK, BLK), :] = total
        return 0

    lax.fori_loop(0, steps, delayed, 0)

    self_v.wait()
    rest = pl.ds(0, DEV - 1)
    pltpu.make_async_copy(recv.at[rest], recv.at[rest], v_recv).wait()
    heard = recv[:, CAP : CAP + 1, :].reshape(DEV, HALF).astype(F32).astype(BF16)
    expand = ((iota((DEV, SLOTS), 1) >> 4) == iota((DEV, SLOTS), 0)).astype(BF16)
    wide = tn(heard, expand)
    line = iota((16, SLOTS), 0)
    mine = line == (iota((16, SLOTS), 1) & 15)

    def picked(first):
        return jnp.sum(jnp.where(mine, wide[first : first + 16, :], 0.0), axis=0, keepdims=True)

    node = (picked(0) * 32.0 + picked(16)).astype(I32)
    weight = picked(32).astype(I32)
    weight = jnp.where(weight > 0, power(weight - 1, -1) * 2.0**-12, 0.0)

    share = acc.shape[0] // COLS
    expand = ((iota((DEV, asks), 1) >> 3) == iota((DEV, asks), 0)).astype(BF16)
    wide = tn(heard, expand)[48:56, :]
    line = iota((span, asks), 0)
    mine = line == (iota((span, asks), 1) & (span - 1))
    place = jnp.sum(jnp.where(mine, wide, 0.0), axis=0, keepdims=True).astype(I32)
    take[...] = (iota((share, asks), 0) == place).astype(BF16)

    def unpack(t, _):
        at = pl.ds(pl.multiple_of(t * chunk, chunk), chunk)
        w = recv[pl.ds(t * (chunk // CAP), chunk // CAP), 0:CAP, :].reshape(chunk, HALF)
        planes[at, 0 * HALF : 1 * HALF] = (w >> 24).astype(F32).astype(BF16)
        planes[at, 1 * HALF : 2 * HALF] = ((w << 16) >> 24).astype(F32).astype(BF16)
        planes[at, 2 * HALF : 3 * HALF] = ((w >> 16) & 255).astype(F32).astype(BF16)
        planes[at, 3 * HALF : 4 * HALF] = (w & 255).astype(F32).astype(BF16)
        return 0

    lax.fori_loop(0, SLOTS // chunk, unpack, 0)
    past_copy.wait()

    xpos, core = row // CORES, lax.rem(row, CORES)
    right, left, far = lax.rem(xpos + 1, XS), lax.rem(xpos + XS - 1, XS), lax.rem(xpos + 2, XS)
    other = 1 - core

    def piece(at_x, at_core, j):
        start = (at_x * CORES + at_core) * OWN + j * PIECE
        return pl.ds(pl.multiple_of(start, PIECE), PIECE)

    def move(at_x, at_core, j, to_x, to_core, sem, recv_sem):
        at = piece(at_x, at_core, j)
        return pltpu.make_async_remote_copy(
            gathered.at[at], gathered.at[at], sem, recv_sem,
            device_id=(to_x * CORES + to_core, col), device_id_type=MESH,
        )

    def arrived(at_x, at_core, j, recv_sem):
        at = piece(at_x, at_core, j)
        pltpu.make_async_copy(gathered.at[at], gathered.at[at], recv_sem).wait()

    def write(at_x, at_core, j):
        at = piece(at_x, at_core, j)
        return pltpu.make_async_copy(gathered.at[at], charge_out.at[at], w_sem.at[at_x * CORES + at_core, j])

    def use(at_x, at_core, j):
        block = (at_x * CORES + at_core) * PIECES + j
        write(at_x, at_core, j).start()
        source = gathered[piece(at_x, at_core, j), :]
        at = pl.ds(pl.multiple_of(lax.rem(j, 2) * BLK, BLK), BLK)
        for i in range(2):
            part = nn(coef[block // 2, pl.ds(i * BLK, BLK), at], source)
            acc[pl.ds(i * BLK, BLK), :] += jnp.where(delays[i, block] == 0, part, 0.0)

    def turn(t):
        return lax.rem(t, 2) * 2 + t // 2

    def settle(t, _):
        j = turn(t)
        spot = iota((PIECE, SLOTS), 0) + j * PIECE
        gate = jnp.where(spot == node, weight, 0.0).astype(BF16)
        both = nn(gate, planes[...])
        rise = both[:, :EXC] * 256.0 + both[:, EXC:]
        fresh = past[pl.ds(pl.multiple_of(j * PIECE, PIECE), PIECE), :].astype(F32) + rise
        gathered[piece(xpos, core, j), :] = fresh.astype(BF16)
        move(xpos, core, j, right, core, g_send.at[0, j], g_near.at[0, j]).start()
        move(xpos, core, j, left, core, g_send.at[1, j], g_near.at[1, j]).start()
        move(xpos, core, j, xpos, other, g_send.at[2, j], g_pair.at[0, j]).start()
        return 0

    lax.fori_loop(0, PIECES, settle, 0)

    def near(t, _):
        j = turn(t)
        arrived(left, core, j, g_near.at[0, j])

        @pl.when(j < 2)
        def _():
            move(left, core, j, right, core, g_send.at[3, j], g_near.at[2, j]).start()

        move(left, core, j, xpos, other, g_send.at[4, j], g_pair.at[1, j]).start()
        use(xpos, core, j)
        arrived(right, core, j, g_near.at[1, j])

        @pl.when(j >= 2)
        def _():
            move(right, core, j, left, core, g_send.at[3, j], g_near.at[2, j]).start()

        move(right, core, j, xpos, other, g_send.at[5, j], g_pair.at[2, j]).start()
        use(left, core, j)
        use(right, core, j)
        arrived(xpos, other, j, g_pair.at[0, j])
        use(xpos, other, j)
        return 0

    lax.fori_loop(0, PIECES, near, 0)

    def distant(t, _):
        j = turn(t)
        arrived(far, core, j, g_near.at[2, j])
        move(far, core, j, xpos, other, g_send.at[6, j], g_pair.at[3, j]).start()
        arrived(left, other, j, g_pair.at[1, j])
        use(left, other, j)
        arrived(right, other, j, g_pair.at[2, j])
        use(right, other, j)
        use(far, core, j)
        return 0

    lax.fori_loop(0, PIECES, distant, 0)

    def last(t, _):
        j = turn(t)
        arrived(far, other, j, g_pair.at[3, j])
        use(far, other, j)
        return 0

    lax.fori_loop(0, PIECES, last, 0)

    def give(t, _):
        to = lax.rem(col + t, COLS)
        value = acc[pl.ds(pl.multiple_of(to * share, share), share), :]
        top = jnp.max(jnp.abs(value), axis=0, keepdims=True)
        up, number = coded(value, top)
        p_send[to, 0:share, :] = word_of(number.astype(I32))
        p_send[to, share : share + 1, :] = up[:, :HALF]
        p_send[to, share + 1 : share + 2, :] = up[:, HALF:]

        @pl.when(t < COLS)
        def _():
            pltpu.make_async_remote_copy(
                p_send.at[to], p_recv.at[col], r_send, r_recv,
                device_id=(row, to), device_id_type=MESH,
            ).start()

        return 0

    lax.fori_loop(1, COLS + 1, give, 0)
    self_p = pltpu.make_async_copy(p_send.at[col], p_recv.at[col], self_sem.at[1])
    self_p.start()
    self_p.wait()
    rest = pl.ds(0, COLS - 1)
    pltpu.make_async_copy(p_recv.at[rest], p_recv.at[rest], r_recv).wait()

    def gain(n, totals):
        w = p_recv[n, 0:share, :]
        factor = power(p_recv[n, share : share + 2, :], 1) * LEAST
        a = totals[0] + (w >> 16).astype(F32) * factor[0:1, :]
        b = totals[1] + ((w << 16) >> 16).astype(F32) * factor[1:2, :]
        return a, b

    zero = jnp.zeros((share, HALF), F32)
    a, b = lax.fori_loop(0, COLS, gain, (zero, zero))

    top = jnp.max(jnp.maximum(jnp.abs(a), jnp.abs(b)), axis=0, keepdims=True)
    up, number_a = coded(a, top)
    number = jnp.concatenate([number_a, coded(b, top)[1]], axis=1)
    answer[:, SCAP : SCAP + 1, :] = jnp.broadcast_to(up.reshape(1, 1, HALF), (DEV, 1, HALF))
    high = jnp.floor(number * (1.0 / 256.0))
    low = (number - high * 256.0).astype(BF16)
    high = high.astype(BF16)
    for g in range(asks // HALF):
        chosen = take[:, g * HALF : (g + 1) * HALF]
        value = (tn(chosen, high) * 256.0 + tn(chosen, low)).astype(I32)
        word = word_of(value).reshape(HALF // span, span, HALF)
        answer[pl.ds(g * (HALF // span), HALF // span), 0:SCAP, :] = word[:, :SCAP, :]

    def send_answer(t, _):
        to = lax.rem(me + t * STRIDE, DEV)
        pltpu.make_async_remote_copy(
            answer.at[to], replies.at[me], a_send, a_recv,
            device_id=device_of(to), device_id_type=MESH,
        ).start()
        return 0

    lax.fori_loop(1, DEV, send_answer, 0)
    self_a = pltpu.make_async_copy(answer.at[me], replies.at[me], self_sem.at[2])
    self_a.start()

    for n in range(7):
        def left_here(j, _):
            at = piece(xpos, core, j)
            pltpu.make_async_copy(gathered.at[at], gathered.at[at], g_send.at[n, j]).wait()
            return 0

        lax.fori_loop(0, PIECES, left_here, 0)

    def written(n, _):
        write(n // CORES // PIECES, lax.rem(n // PIECES, CORES), lax.rem(n, PIECES)).wait()
        return 0

    lax.fori_loop(0, ROWS * PIECES, written, 0)
    rest = pl.ds(0, DEV - 1)
    pltpu.make_async_copy(send.at[rest], send.at[rest], v_send).wait()
    rest = pl.ds(0, COLS - 1)
    pltpu.make_async_copy(p_send.at[rest], p_send.at[rest], r_send).wait()
    self_a.wait()
    rest = pl.ds(0, DEV - 1)
    pltpu.make_async_copy(replies.at[rest], replies.at[rest], a_recv).wait()
    pltpu.make_async_copy(answer.at[rest], answer.at[rest], a_send).wait()


def emit_kernel(charge, replies, sowner, charge_now, drops, block, in_sem, out_sem):
    span = charge.shape[0] // 8

    def load(part):
        at = pl.ds(part * span, span)
        return pltpu.make_async_copy(charge.at[at], block.at[at], in_sem.at[part])

    def save(part):
        at = pl.ds(part * span, span)
        return pltpu.make_async_copy(block.at[at], charge_now.at[at], out_sem.at[part])

    for part in range(8):
        load(part).start()
    s_own = sowner[...]
    s_from, s_to = s_own[0:1, :], s_own[1:2, :]
    _, _, s_0, s_1 = ranks_of(s_from, s_to)
    wide = 2 * SCAP
    asks = DEV * wide
    line = iota((asks, s_own.shape[1]), 0)
    gate = (line == s_from * wide + s_0).astype(F32) - (line == s_to * wide + s_1).astype(F32)
    gate = gate.astype(BF16)
    for part in range(8):
        load(part).wait()
        save(part).start()
    w = replies[:, 0:SCAP, :]
    up = replies[:, SCAP : SCAP + 1, :].reshape(DEV, HALF)
    factor = (power(up, 1) * LEAST).reshape(DEV, 1, HALF)
    for half in range(2):
        number = (w >> 16) if half == 0 else ((w << 16) >> 16)
        value = number.astype(F32) * factor
        value = jnp.concatenate([value, value], axis=1).reshape(asks, HALF)
        high, low = split(value)
        drops[:, half * HALF : (half + 1) * HALF] = tn(gate, high) + tn(gate, low)
    for part in range(8):
        save(part).wait()


def emit(charge, replies, sowner):
    vmem, hbm = pl.BlockSpec(memory_space=pltpu.VMEM), pl.BlockSpec(memory_space=pl.ANY)
    dma = pltpu.SemaphoreType.DMA
    return pl.pallas_call(
        emit_kernel,
        out_shape=(
            jax.ShapeDtypeStruct(charge.shape, BF16),
            jax.ShapeDtypeStruct((sowner.shape[1], EXC), F32),
        ),
        in_specs=[hbm, vmem, vmem],
        out_specs=(hbm, vmem),
        scratch_shapes=[pltpu.VMEM(charge.shape, BF16), dma((8,)), dma((8,))],
        compiler_params=pltpu.CompilerParams(vmem_limit_bytes=FULL),
        name="emit",
    )(charge, replies, sowner)


def split(value):
    top = value.astype(BF16)
    return top, (value - top.astype(F32)).astype(BF16)


def step(cur, owner, slot, sowner, soffset, hist, coef, delays):
    hbm = pl.BlockSpec(memory_space=pl.ANY)
    nodes, rows = hist.shape[1], coef.shape[0]
    width = 2 * BLK
    dma = pltpu.SemaphoreType.DMA
    asks = DEV * 2 * SCAP
    return pl.pallas_call(
        step_kernel,
        out_shape=(
            jax.ShapeDtypeStruct((nodes, EXC), BF16),
            jax.ShapeDtypeStruct((DEV, SCAP + 1, HALF), I32),
        ),
        in_specs=[hbm] * 8,
        out_specs=(hbm, hbm),
        scratch_shapes=[
            pltpu.VMEM(cur.shape, F32),
            pltpu.VMEM(owner.shape, I32),
            pltpu.VMEM(slot.shape, I32),
            pltpu.VMEM(sowner.shape, I32),
            pltpu.VMEM(soffset.shape, I32),
            pltpu.SMEM(delays.shape, I32),
            pltpu.VMEM((DEV, CAP + 1, HALF), I32),
            pltpu.VMEM((DEV, CAP + 1, HALF), I32),
            pltpu.VMEM((SLOTS, 2 * EXC), BF16),
            pltpu.VMEM((BRANCH, EXC), BF16),
            pltpu.VMEM((BRANCH, EXC), BF16),
            pltpu.VMEM((OWN, EXC), BF16),
            pltpu.VMEM((nodes // width, rows, width), BF16),
            pltpu.VMEM(hist.shape, BF16),
            pltpu.VMEM((rows, EXC), F32),
            pltpu.VMEM((nodes, EXC), BF16),
            pltpu.VMEM((rows // COLS, asks), BF16),
            pltpu.VMEM((COLS, rows // COLS + 2, HALF), I32),
            pltpu.VMEM((COLS, rows // COLS + 2, HALF), I32),
            pltpu.VMEM((DEV, SCAP + 1, HALF), I32),
            dma((6,)), dma, dma, dma((3,)), dma, dma, dma((nodes // width,)), dma((ROWS, PIECES)),
            dma((7, PIECES)), dma((3, PIECES)), dma((4, PIECES)),
            dma, dma, dma, dma,
        ],
        compiler_params=pltpu.CompilerParams(
            collective_id=0, has_side_effects=True, vmem_limit_bytes=FULL
        ),
        name="step",
    )(cur, owner, slot, sowner, soffset, hist, coef, delays)


def local(
    currents, branch_owner, branch_slot, history, coefficients, delays, slab_owner, slab_offset
):
    sowner = slab_owner.T
    charge, replies = step(
        currents, branch_owner.T, branch_slot.T, sowner, slab_offset.T, history, coefficients, delays
    )
    return emit(charge, replies, sowner)


def solution(mesh):
    placed = (
        P(("row", "col"), None),
        P(("row", "col"), None),
        P(("row", "col"), None),
        P(None, "col", None),
        P("row", "col"),
        P("row", "col"),
        P(("row", "col"), None),
        P(("row", "col"), None),
    )
    return jax.shard_map(
        local,
        mesh=mesh,
        in_specs=placed,
        out_specs=(P("col", None), P(("row", "col"), None)),
        check_vma=False,
    )
```

```python
import functools

import jax
import jax.numpy as jnp
from jax import lax
from jax.experimental import pallas as pl
from jax.experimental.pallas import tpu as pltpu
from jax.sharding import PartitionSpec as P

F32 = jnp.float32
BF16 = jnp.bfloat16
I32 = jnp.int32
MESH = pl.DeviceIdType.MESH

ROWS = 8
COLS = 16
DEV = ROWS * COLS
CORES = 2
XS = ROWS // CORES
BRANCH = 256
CAP = 16
SCAP = 4
OWN = 1024
EXC = 256
HALF = 128
SLOTS = DEV * CAP
BLK = 256
PIECES = 4
PIECE = OWN // PIECES
FULL = 67043328
STRIDE = 1
LEAST = 2.0**-80


def iota(shape, dim):
    return lax.broadcasted_iota(I32, shape, dim)


def nn(a, b):
    return lax.dot_general(a, b, (((1,), (0,)), ((), ())), preferred_element_type=F32)


def nt(a, b):
    return lax.dot_general(a, b, (((1,), (1,)), ((), ())), preferred_element_type=F32)


def tn(a, b):
    return lax.dot_general(a, b, (((0,), (0,)), ((), ())), preferred_element_type=F32)


def power(exponent, sign):
    result = jnp.ones(exponent.shape, F32)
    for bit in range(7):
        factor = 2.0 ** (sign * (1 << bit))
        result = result * jnp.where(((exponent >> bit) & 1) > 0, factor, 1.0)
    return result


def coded(value, top):
    up = jnp.zeros(top.shape, I32)
    unit = jnp.full(top.shape, LEAST, F32)
    inverse = jnp.full(top.shape, 1.0 / LEAST, F32)
    for bit in (6, 5, 4, 3, 2, 1, 0):
        leap = 1 << bit
        larger = top > unit * (32766.0 * 2.0 ** (leap - 1))
        up = jnp.where(larger, up + leap, up)
        unit = jnp.where(larger, unit * 2.0**leap, unit)
        inverse = jnp.where(larger, inverse * 2.0**-leap, inverse)
    return up, jnp.round(value * inverse)


def device_of(index):
    return (index // COLS, lax.rem(index, COLS))


def ranks_of(first, second):
    n = first.shape[1]
    hot_a = iota((DEV, n), 0) == first
    hot_b = iota((DEV, n), 0) == second
    a, b = hot_a.astype(F32), hot_b.astype(F32)
    before = (iota((n, n), 0) < iota((n, n), 1)).astype(BF16)
    seen_a = nn(a.astype(BF16), before)
    seen_b = nn(b.astype(BF16), before) + jnp.sum(a, axis=1, keepdims=True)
    rank_a = jnp.sum(a * seen_a, axis=0, keepdims=True).astype(I32)
    rank_b = jnp.sum(b * seen_b, axis=0, keepdims=True).astype(I32)
    return a.astype(BF16), b.astype(BF16), rank_a, rank_b


def greet(row, col):
    barrier = pltpu.get_barrier_semaphore()

    def down(t, _):
        there = (lax.rem(row + t, ROWS), col)
        pl.semaphore_signal(barrier, inc=1, device_id=there, device_id_type=MESH)
        return 0

    def along(t, _):
        there = (row, lax.rem(col + t, COLS))
        pl.semaphore_signal(barrier, inc=1, device_id=there, device_id_type=MESH)
        return 0

    lax.fori_loop(1, ROWS, down, 0)
    lax.fori_loop(1, COLS, along, 0)
    return barrier


def step_kernel(
    cur_h, owner_h, slot_h, sowner_h, soffset_h, hist, coef_h, delays_h,
    charge_out, replies,
    cur, owner, slot, sowner, soffset, delays,
    send, recv, planes, q_hi, q_lo, past, coef, held, acc, gathered,
    take, p_send, p_recv, answer,
    first_sem, v_send, v_recv, self_sem, past_sem, h_sem, c_sem, w_sem,
    g_send, g_near, g_pair, r_send, r_recv, a_send, a_recv, ready,
):
    row, col = lax.axis_index("row"), lax.axis_index("col")
    me = row * COLS + col
    barrier = greet(row, col)
    small = ((cur_h, cur), (owner_h, owner), (slot_h, slot), (sowner_h, sowner), (soffset_h, soffset), (delays_h, delays))
    small = [pltpu.make_async_copy(a, b, first_sem.at[n]) for n, (a, b) in enumerate(small)]
    for copy in small:
        copy.start()
    past_copy = pltpu.make_async_copy(hist.at[0, pl.ds(pl.multiple_of(row * OWN, OWN), OWN)], past, past_sem)
    past_copy.start()

    width = 2 * BLK
    steps = coef.shape[0]

    def fetch(step):
        at = pl.ds(pl.multiple_of(step * width, width), width)
        return (
            pltpu.make_async_copy(hist.at[:, at], held.at[:, at], h_sem),
            pltpu.make_async_copy(coef_h.at[:, at], coef.at[step], c_sem.at[step]),
        )

    def bring(step, _):
        for copy in fetch(step):
            copy.start()
        return 0

    lax.fori_loop(0, steps, bring, 0)
    for copy in small:
        copy.wait()

    own = owner[...]
    targets = (own & (ROWS - 1)) * COLS + (own >> 3)
    t_from, t_to = targets[0:1, :], targets[1:2, :]
    hot_from, hot_to, r_from, r_to = ranks_of(t_from, t_to)
    p_from, p_to = t_from * CAP + r_from, t_to * CAP + r_to
    x = cur[...]
    size = jnp.abs(x)
    size = jnp.maximum(size[:, :HALF], size[:, HALF:])
    largest = jnp.max(size.T, axis=0, keepdims=True)
    scale = jnp.full((1, BRANCH), 2.0**-12, F32)
    inverse = jnp.full((1, BRANCH), 2.0**12, F32)
    exponent = jnp.ones((1, BRANCH), F32)
    for _ in range(32):
        smaller = largest <= scale * 16383.0
        scale = jnp.where(smaller, scale * 0.5, scale)
        inverse = jnp.where(smaller, inverse * 2.0, inverse)
        exponent = jnp.where(smaller, exponent + 1.0, exponent)
    spread = jnp.broadcast_to(inverse, (HALF, BRANCH)).T
    q = jnp.round(x * jnp.concatenate([spread, spread], axis=1))
    high = jnp.floor(q * (1.0 / 256.0))
    q_hi[...] = high.astype(BF16)
    q_lo[...] = (q - high * 256.0).astype(BF16)

    def told(rank, number):
        line = iota((HALF, BRANCH), 0)
        words = jnp.where(line == rank, (number >> 5).astype(F32), 0.0)
        words = words + jnp.where(line == rank + 16, (number & 31).astype(F32), 0.0)
        return (words + jnp.where(line == rank + 32, exponent, 0.0)).astype(BF16)

    s_own, s_off = sowner[...], soffset[...]
    s_from, s_to = s_own[0:1, :], s_own[1:2, :]
    hot_0, hot_1, s_0, s_1 = ranks_of(s_from, s_to)

    def asked(rank, offset):
        line = iota((HALF, offset.shape[1]), 0)
        return jnp.where(line == rank + 48, offset.astype(F32), 0.0).astype(BF16)

    slots = slot[...]
    words = nt(hot_from, told(r_from, slots[0:1, :])) + nt(hot_to, told(r_to, slots[1:2, :]))
    words = words + nt(hot_0, asked(s_0, s_off[0:1, :])) + nt(hot_1, asked(s_1, s_off[1:2, :]))
    send[:, CAP : CAP + 1, :] = words.astype(I32).reshape(DEV, 1, HALF)

    chunk = 256

    def word_of(value):
        return (value[:, :HALF] << 16) | (value[:, HALF:] & 0xFFFF)

    def fill(t, _):
        place = iota((chunk, BRANCH), 0) + t * chunk
        sign = (place == p_to).astype(F32) - (place == p_from).astype(F32)
        sign = sign.astype(BF16)
        value = (nn(sign, q_hi[...]) * 256.0 + nn(sign, q_lo[...])).astype(I32)
        word = word_of(value).reshape(chunk // CAP, CAP, HALF)
        send[pl.ds(t * (chunk // CAP), chunk // CAP), 0:CAP, :] = word
        return 0

    pl.semaphore_wait(barrier, ROWS - 1 + COLS - 1)

    def pass_on(t, _):
        there = (lax.rem(row + t, ROWS), col)
        pl.semaphore_signal(ready, inc=1, device_id=there, device_id_type=MESH)
        return 0

    lax.fori_loop(1, ROWS, pass_on, 0)
    lax.fori_loop(0, SLOTS // chunk, fill, 0)
    pl.semaphore_wait(ready, ROWS - 1)

    def out(t, _):
        other = lax.rem(me + t * STRIDE, DEV)
        pltpu.make_async_remote_copy(
            send.at[other], recv.at[me], v_send, v_recv,
            device_id=device_of(other), device_id_type=MESH,
        ).start()
        return 0

    lax.fori_loop(1, DEV, out, 0)
    self_v = pltpu.make_async_copy(send.at[me], recv.at[me], self_sem.at[0])
    self_v.start()
    span = 2 * SCAP
    asks = DEV * span

    acc[...] = jnp.zeros_like(acc)

    def landed(step, _):
        for copy in fetch(step):
            copy.wait()
        return 0

    lax.fori_loop(0, steps, landed, 0)

    def delayed(step, _):
        for i in range(2):
            total = acc[pl.ds(i * BLK, BLK), :]
            for k in range(2):
                d = delays[i, step * 2 + k]
                at = pl.ds(pl.multiple_of(step * width + k * BLK, BLK), BLK)
                source = held[jnp.maximum(d - 1, 0), at, :]
                part = nn(coef[step, pl.ds(i * BLK, BLK), pl.ds(k * BLK, BLK)], source)
                total = total + jnp.where(d > 0, part, 0.0)
            acc[pl.ds(i * BLK, BLK), :] = total
        return 0

    lax.fori_loop(0, steps, delayed, 0)

    self_v.wait()
    rest = pl.ds(0, DEV - 1)
    pltpu.make_async_copy(recv.at[rest], recv.at[rest], v_recv).wait()
    heard = recv[:, CAP : CAP + 1, :].reshape(DEV, HALF).astype(F32).astype(BF16)
    expand = ((iota((DEV, SLOTS), 1) >> 4) == iota((DEV, SLOTS), 0)).astype(BF16)
    wide = tn(heard, expand)
    line = iota((16, SLOTS), 0)
    mine = line == (iota((16, SLOTS), 1) & 15)

    def picked(first):
        return jnp.sum(jnp.where(mine, wide[first : first + 16, :], 0.0), axis=0, keepdims=True)

    node = (picked(0) * 32.0 + picked(16)).astype(I32)
    weight = picked(32).astype(I32)
    weight = jnp.where(weight > 0, power(weight - 1, -1) * 2.0**-12, 0.0)

    share = acc.shape[0] // COLS
    expand = ((iota((DEV, asks), 1) >> 3) == iota((DEV, asks), 0)).astype(BF16)
    wide = tn(heard, expand)[48:56, :]
    line = iota((span, asks), 0)
    mine = line == (iota((span, asks), 1) & (span - 1))
    place = jnp.sum(jnp.where(mine, wide, 0.0), axis=0, keepdims=True).astype(I32)
    take[...] = (iota((share, asks), 0) == place).astype(BF16)

    def unpack(t, _):
        at = pl.ds(pl.multiple_of(t * chunk, chunk), chunk)
        w = recv[pl.ds(t * (chunk // CAP), chunk // CAP), 0:CAP, :].reshape(chunk, HALF)
        planes[at, 0 * HALF : 1 * HALF] = (w >> 24).astype(F32).astype(BF16)
        planes[at, 1 * HALF : 2 * HALF] = ((w << 16) >> 24).astype(F32).astype(BF16)
        planes[at, 2 * HALF : 3 * HALF] = ((w >> 16) & 255).astype(F32).astype(BF16)
        planes[at, 3 * HALF : 4 * HALF] = (w & 255).astype(F32).astype(BF16)
        return 0

    lax.fori_loop(0, SLOTS // chunk, unpack, 0)
    past_copy.wait()

    xpos, core = row // CORES, lax.rem(row, CORES)
    right, left, far = lax.rem(xpos + 1, XS), lax.rem(xpos + XS - 1, XS), lax.rem(xpos + 2, XS)
    other = 1 - core

    def piece(at_x, at_core, j):
        start = (at_x * CORES + at_core) * OWN + j * PIECE
        return pl.ds(pl.multiple_of(start, PIECE), PIECE)

    def move(at_x, at_core, j, to_x, to_core, sem, recv_sem):
        at = piece(at_x, at_core, j)
        return pltpu.make_async_remote_copy(
            gathered.at[at], gathered.at[at], sem, recv_sem,
            device_id=(to_x * CORES + to_core, col), device_id_type=MESH,
        )

    def arrived(at_x, at_core, j, recv_sem):
        at = piece(at_x, at_core, j)
        pltpu.make_async_copy(gathered.at[at], gathered.at[at], recv_sem).wait()

    def write(at_x, at_core, j):
        at = piece(at_x, at_core, j)
        return pltpu.make_async_copy(gathered.at[at], charge_out.at[at], w_sem.at[at_x * CORES + at_core, j])

    def use(at_x, at_core, j):
        block = (at_x * CORES + at_core) * PIECES + j
        write(at_x, at_core, j).start()
        source = gathered[piece(at_x, at_core, j), :]
        at = pl.ds(pl.multiple_of(lax.rem(j, 2) * BLK, BLK), BLK)
        for i in range(2):
            part = nn(coef[block // 2, pl.ds(i * BLK, BLK), at], source)
            acc[pl.ds(i * BLK, BLK), :] += jnp.where(delays[i, block] == 0, part, 0.0)

    def turn(t):
        return lax.rem(t, 2) * 2 + t // 2

    def settle(t, _):
        j = turn(t)
        spot = iota((PIECE, SLOTS), 0) + j * PIECE
        gate = jnp.where(spot == node, weight, 0.0).astype(BF16)
        both = nn(gate, planes[...])
        rise = both[:, :EXC] * 256.0 + both[:, EXC:]
        fresh = past[pl.ds(pl.multiple_of(j * PIECE, PIECE), PIECE), :].astype(F32) + rise
        gathered[piece(xpos, core, j), :] = fresh.astype(BF16)
        move(xpos, core, j, right, core, g_send.at[0, j], g_near.at[0, j]).start()
        move(xpos, core, j, left, core, g_send.at[1, j], g_near.at[1, j]).start()
        move(xpos, core, j, xpos, other, g_send.at[2, j], g_pair.at[0, j]).start()
        return 0

    lax.fori_loop(0, PIECES, settle, 0)

    def near(t, _):
        j = turn(t)
        arrived(left, core, j, g_near.at[0, j])

        @pl.when(j < 2)
        def _():
            move(left, core, j, right, core, g_send.at[3, j], g_near.at[2, j]).start()

        move(left, core, j, xpos, other, g_send.at[4, j], g_pair.at[1, j]).start()
        use(xpos, core, j)
        arrived(right, core, j, g_near.at[1, j])

        @pl.when(j >= 2)
        def _():
            move(right, core, j, left, core, g_send.at[3, j], g_near.at[2, j]).start()

        move(right, core, j, xpos, other, g_send.at[5, j], g_pair.at[2, j]).start()
        use(left, core, j)
        use(right, core, j)
        arrived(xpos, other, j, g_pair.at[0, j])
        use(xpos, other, j)
        return 0

    lax.fori_loop(0, PIECES, near, 0)

    def distant(t, _):
        j = turn(t)
        arrived(far, core, j, g_near.at[2, j])
        move(far, core, j, xpos, other, g_send.at[6, j], g_pair.at[3, j]).start()
        arrived(left, other, j, g_pair.at[1, j])
        use(left, other, j)
        arrived(right, other, j, g_pair.at[2, j])
        use(right, other, j)
        use(far, core, j)
        return 0

    lax.fori_loop(0, PIECES, distant, 0)

    def last(t, _):
        j = turn(t)
        arrived(far, other, j, g_pair.at[3, j])
        use(far, other, j)
        return 0

    lax.fori_loop(0, PIECES, last, 0)

    def give(t, _):
        to = lax.rem(col + t, COLS)
        value = acc[pl.ds(pl.multiple_of(to * share, share), share), :]
        top = jnp.max(jnp.abs(value), axis=0, keepdims=True)
        up, number = coded(value, top)
        p_send[to, 0:share, :] = word_of(number.astype(I32))
        p_send[to, share : share + 1, :] = up[:, :HALF]
        p_send[to, share + 1 : share + 2, :] = up[:, HALF:]

        @pl.when(t < COLS)
        def _():
            pltpu.make_async_remote_copy(
                p_send.at[to], p_recv.at[col], r_send, r_recv,
                device_id=(row, to), device_id_type=MESH,
            ).start()

        return 0

    lax.fori_loop(1, COLS + 1, give, 0)
    self_p = pltpu.make_async_copy(p_send.at[col], p_recv.at[col], self_sem.at[1])
    self_p.start()
    self_p.wait()
    rest = pl.ds(0, COLS - 1)
    pltpu.make_async_copy(p_recv.at[rest], p_recv.at[rest], r_recv).wait()

    def gain(n, totals):
        w = p_recv[n, 0:share, :]
        factor = power(p_recv[n, share : share + 2, :], 1) * LEAST
        a = totals[0] + (w >> 16).astype(F32) * factor[0:1, :]
        b = totals[1] + ((w << 16) >> 16).astype(F32) * factor[1:2, :]
        return a, b

    zero = jnp.zeros((share, HALF), F32)
    a, b = lax.fori_loop(0, COLS, gain, (zero, zero))

    top = jnp.max(jnp.maximum(jnp.abs(a), jnp.abs(b)), axis=0, keepdims=True)
    up, number_a = coded(a, top)
    number = jnp.concatenate([number_a, coded(b, top)[1]], axis=1)
    answer[:, SCAP : SCAP + 1, :] = jnp.broadcast_to(up.reshape(1, 1, HALF), (DEV, 1, HALF))
    high = jnp.floor(number * (1.0 / 256.0))
    low = (number - high * 256.0).astype(BF16)
    high = high.astype(BF16)
    for g in range(asks // HALF):
        chosen = take[:, g * HALF : (g + 1) * HALF]
        value = (tn(chosen, high) * 256.0 + tn(chosen, low)).astype(I32)
        word = word_of(value).reshape(HALF // span, span, HALF)
        answer[pl.ds(g * (HALF // span), HALF // span), 0:SCAP, :] = word[:, :SCAP, :]

    def send_answer(t, _):
        to = lax.rem(me + t * STRIDE, DEV)
        pltpu.make_async_remote_copy(
            answer.at[to], replies.at[me], a_send, a_recv,
            device_id=device_of(to), device_id_type=MESH,
        ).start()
        return 0

    lax.fori_loop(1, DEV, send_answer, 0)
    self_a = pltpu.make_async_copy(answer.at[me], replies.at[me], self_sem.at[2])
    self_a.start()

    for n in range(7):
        def left_here(j, _):
            at = piece(xpos, core, j)
            pltpu.make_async_copy(gathered.at[at], gathered.at[at], g_send.at[n, j]).wait()
            return 0

        lax.fori_loop(0, PIECES, left_here, 0)

    def written(n, _):
        write(n // CORES // PIECES, lax.rem(n // PIECES, CORES), lax.rem(n, PIECES)).wait()
        return 0

    lax.fori_loop(0, ROWS * PIECES, written, 0)
    rest = pl.ds(0, DEV - 1)
    pltpu.make_async_copy(send.at[rest], send.at[rest], v_send).wait()
    rest = pl.ds(0, COLS - 1)
    pltpu.make_async_copy(p_send.at[rest], p_send.at[rest], r_send).wait()
    self_a.wait()
    rest = pl.ds(0, DEV - 1)
    pltpu.make_async_copy(replies.at[rest], replies.at[rest], a_recv).wait()
    pltpu.make_async_copy(answer.at[rest], answer.at[rest], a_send).wait()


def emit_kernel(
    charge, replies_h, sowner_h, charge_now, drops, block, replies, sowner, in_sem, out_sem, small_sem
):
    span = charge.shape[0] // 8

    def load(part):
        at = pl.ds(part * span, span)
        return pltpu.make_async_copy(charge.at[at], block.at[at], in_sem.at[part])

    def save(part):
        at = pl.ds(part * span, span)
        return pltpu.make_async_copy(block.at[at], charge_now.at[at], out_sem.at[part])

    few = pltpu.make_async_copy(sowner_h, sowner, small_sem.at[0])
    told = pltpu.make_async_copy(replies_h, replies, small_sem.at[1])
    few.start()
    for part in range(8):
        load(part).start()
    told.start()
    few.wait()
    s_own = sowner[...]
    s_from, s_to = s_own[0:1, :], s_own[1:2, :]
    _, _, s_0, s_1 = ranks_of(s_from, s_to)
    wide = 2 * SCAP
    asks = DEV * wide
    line = iota((asks, s_own.shape[1]), 0)
    gate = (line == s_from * wide + s_0).astype(F32) - (line == s_to * wide + s_1).astype(F32)
    gate = gate.astype(BF16)
    for part in range(8):
        load(part).wait()
        save(part).start()
    told.wait()
    w = replies[:, 0:SCAP, :]
    up = replies[:, SCAP : SCAP + 1, :].reshape(DEV, HALF)
    factor = (power(up, 1) * LEAST).reshape(DEV, 1, HALF)
    for half in range(2):
        number = (w >> 16) if half == 0 else ((w << 16) >> 16)
        value = number.astype(F32) * factor
        value = jnp.concatenate([value, value], axis=1).reshape(asks, HALF)
        high, low = split(value)
        drops[:, half * HALF : (half + 1) * HALF] = tn(gate, high) + tn(gate, low)
    for part in range(8):
        save(part).wait()


def emit(charge, replies, sowner):
    vmem, hbm = pl.BlockSpec(memory_space=pltpu.VMEM), pl.BlockSpec(memory_space=pl.ANY)
    dma = pltpu.SemaphoreType.DMA
    return pl.pallas_call(
        emit_kernel,
        out_shape=(
            jax.ShapeDtypeStruct(charge.shape, BF16),
            jax.ShapeDtypeStruct((sowner.shape[1], EXC), F32),
        ),
        in_specs=[hbm, hbm, hbm],
        out_specs=(hbm, vmem),
        scratch_shapes=[
            pltpu.VMEM(charge.shape, BF16),
            pltpu.VMEM(replies.shape, I32),
            pltpu.VMEM(sowner.shape, I32),
            dma((8,)), dma((8,)), dma((2,)),
        ],
        compiler_params=pltpu.CompilerParams(vmem_limit_bytes=FULL),
        name="emit",
    )(charge, replies, sowner)


def split(value):
    top = value.astype(BF16)
    return top, (value - top.astype(F32)).astype(BF16)


def step(cur, owner, slot, sowner, soffset, hist, coef, delays):
    hbm = pl.BlockSpec(memory_space=pl.ANY)
    nodes, rows = hist.shape[1], coef.shape[0]
    width = 2 * BLK
    dma = pltpu.SemaphoreType.DMA
    asks = DEV * 2 * SCAP
    return pl.pallas_call(
        step_kernel,
        out_shape=(
            jax.ShapeDtypeStruct((nodes, EXC), BF16),
            jax.ShapeDtypeStruct((DEV, SCAP + 1, HALF), I32),
        ),
        in_specs=[hbm] * 8,
        out_specs=(hbm, hbm),
        scratch_shapes=[
            pltpu.VMEM(cur.shape, F32),
            pltpu.VMEM(owner.shape, I32),
            pltpu.VMEM(slot.shape, I32),
            pltpu.VMEM(sowner.shape, I32),
            pltpu.VMEM(soffset.shape, I32),
            pltpu.SMEM(delays.shape, I32),
            pltpu.VMEM((DEV, CAP + 1, HALF), I32),
            pltpu.VMEM((DEV, CAP + 1, HALF), I32),
            pltpu.VMEM((SLOTS, 2 * EXC), BF16),
            pltpu.VMEM((BRANCH, EXC), BF16),
            pltpu.VMEM((BRANCH, EXC), BF16),
            pltpu.VMEM((OWN, EXC), BF16),
            pltpu.VMEM((nodes // width, rows, width), BF16),
            pltpu.VMEM(hist.shape, BF16),
            pltpu.VMEM((rows, EXC), F32),
            pltpu.VMEM((nodes, EXC), BF16),
            pltpu.VMEM((rows // COLS, asks), BF16),
            pltpu.VMEM((COLS, rows // COLS + 2, HALF), I32),
            pltpu.VMEM((COLS, rows // COLS + 2, HALF), I32),
            pltpu.VMEM((DEV, SCAP + 1, HALF), I32),
            dma((6,)), dma, dma, dma((3,)), dma, dma, dma((nodes // width,)), dma((ROWS, PIECES)),
            dma((7, PIECES)), dma((3, PIECES)), dma((4, PIECES)),
            dma, dma, dma, dma, pltpu.SemaphoreType.REGULAR,
        ],
        compiler_params=pltpu.CompilerParams(
            collective_id=0, has_side_effects=True, vmem_limit_bytes=FULL
        ),
        name="step",
    )(cur, owner, slot, sowner, soffset, hist, coef, delays)


def local(
    currents, branch_owner, branch_slot, history, coefficients, delays, slab_owner, slab_offset
):
    sowner = slab_owner.T
    charge, replies = step(
        currents, branch_owner.T, branch_slot.T, sowner, slab_offset.T, history, coefficients, delays
    )
    return emit(charge, replies, sowner)


def solution(mesh):
    placed = (
        P(("row", "col"), None),
        P(("row", "col"), None),
        P(("row", "col"), None),
        P(None, "col", None),
        P("row", "col"),
        P("row", "col"),
        P(("row", "col"), None),
        P(("row", "col"), None),
    )
    return jax.shard_map(
        local,
        mesh=mesh,
        in_specs=placed,
        out_specs=(P("col", None), P(("row", "col"), None)),
        check_vma=False,
    )
```

```python
import functools

import jax
import jax.numpy as jnp
from jax import lax
from jax.experimental import pallas as pl
from jax.experimental.pallas import tpu as pltpu
from jax.sharding import PartitionSpec as P

F32 = jnp.float32
BF16 = jnp.bfloat16
I32 = jnp.int32
MESH = pl.DeviceIdType.MESH

ROWS = 8
COLS = 16
DEV = ROWS * COLS
CORES = 2
XS = ROWS // CORES
BRANCH = 256
CAP = 16
SCAP = 4
OWN = 1024
EXC = 256
HALF = 128
SLOTS = DEV * CAP
BLK = 256
PIECES = 4
PIECE = OWN // PIECES
FULL = 67043328
STRIDE = 1
LEAST = 2.0**-80


def iota(shape, dim):
    return lax.broadcasted_iota(I32, shape, dim)


def nn(a, b):
    return lax.dot_general(a, b, (((1,), (0,)), ((), ())), preferred_element_type=F32)


def nt(a, b):
    return lax.dot_general(a, b, (((1,), (1,)), ((), ())), preferred_element_type=F32)


def tn(a, b):
    return lax.dot_general(a, b, (((0,), (0,)), ((), ())), preferred_element_type=F32)


def power(exponent, sign):
    result = jnp.ones(exponent.shape, F32)
    for bit in range(7):
        factor = 2.0 ** (sign * (1 << bit))
        result = result * jnp.where(((exponent >> bit) & 1) > 0, factor, 1.0)
    return result


def coded(value, top):
    up = jnp.zeros(top.shape, I32)
    unit = jnp.full(top.shape, LEAST, F32)
    inverse = jnp.full(top.shape, 1.0 / LEAST, F32)
    for bit in (6, 5, 4, 3, 2, 1, 0):
        leap = 1 << bit
        larger = top > unit * (32766.0 * 2.0 ** (leap - 1))
        up = jnp.where(larger, up + leap, up)
        unit = jnp.where(larger, unit * 2.0**leap, unit)
        inverse = jnp.where(larger, inverse * 2.0**-leap, inverse)
    return up, jnp.round(value * inverse)


def device_of(index):
    return (index // COLS, lax.rem(index, COLS))


def ranks_of(first, second):
    n = first.shape[1]
    hot_a = iota((DEV, n), 0) == first
    hot_b = iota((DEV, n), 0) == second
    a, b = hot_a.astype(F32), hot_b.astype(F32)
    before = (iota((n, n), 0) < iota((n, n), 1)).astype(BF16)
    seen_a = nn(a.astype(BF16), before)
    seen_b = nn(b.astype(BF16), before) + jnp.sum(a, axis=1, keepdims=True)
    rank_a = jnp.sum(a * seen_a, axis=0, keepdims=True).astype(I32)
    rank_b = jnp.sum(b * seen_b, axis=0, keepdims=True).astype(I32)
    return a.astype(BF16), b.astype(BF16), rank_a, rank_b


def greet(row, col):
    barrier = pltpu.get_barrier_semaphore()

    def down(t, _):
        there = (lax.rem(row + t, ROWS), col)
        pl.semaphore_signal(barrier, inc=1, device_id=there, device_id_type=MESH)
        return 0

    def along(t, _):
        there = (row, lax.rem(col + t, COLS))
        pl.semaphore_signal(barrier, inc=1, device_id=there, device_id_type=MESH)
        return 0

    lax.fori_loop(1, ROWS, down, 0)
    lax.fori_loop(1, COLS, along, 0)
    return barrier


def step_kernel(
    cur_h, owner_h, slot_h, sowner_h, soffset_h, hist, coef_h, delays_h,
    charge_out, replies,
    cur, owner, slot, sowner, soffset, delays,
    send, recv, planes, q_hi, q_lo, past, coef, held, acc, gathered,
    take, p_send, p_recv, answer,
    first_sem, v_send, v_recv, self_sem, past_sem, h_sem, c_sem, w_sem,
    g_send, g_near, g_pair, r_send, r_recv, a_send, a_recv, ready,
):
    row, col = lax.axis_index("row"), lax.axis_index("col")
    me = row * COLS + col
    barrier = greet(row, col)
    small = ((cur_h, cur), (owner_h, owner), (slot_h, slot), (sowner_h, sowner), (soffset_h, soffset), (delays_h, delays))
    small = [pltpu.make_async_copy(a, b, first_sem.at[n]) for n, (a, b) in enumerate(small)]
    for copy in small:
        copy.start()
    past_copy = pltpu.make_async_copy(hist.at[0, pl.ds(pl.multiple_of(row * OWN, OWN), OWN)], past, past_sem)
    past_copy.start()

    width = 2 * BLK
    steps = coef.shape[0]

    def fetch(step):
        at = pl.ds(pl.multiple_of(step * width, width), width)
        return (
            pltpu.make_async_copy(hist.at[:, at], held.at[:, at], h_sem),
            pltpu.make_async_copy(coef_h.at[:, at], coef.at[step], c_sem.at[step]),
        )

    def bring(step, _):
        for copy in fetch(step):
            copy.start()
        return 0

    lax.fori_loop(0, steps, bring, 0)
    for copy in small:
        copy.wait()

    own = owner[...]
    targets = (own & (ROWS - 1)) * COLS + (own >> 3)
    t_from, t_to = targets[0:1, :], targets[1:2, :]
    hot_from, hot_to, r_from, r_to = ranks_of(t_from, t_to)
    p_from, p_to = t_from * CAP + r_from, t_to * CAP + r_to
    x = cur[...]
    size = jnp.abs(x)
    size = jnp.maximum(size[:, :HALF], size[:, HALF:])
    largest = jnp.max(size.T, axis=0, keepdims=True)
    scale = jnp.full((1, BRANCH), 2.0**-12, F32)
    inverse = jnp.full((1, BRANCH), 2.0**12, F32)
    exponent = jnp.ones((1, BRANCH), F32)
    for _ in range(32):
        smaller = largest <= scale * 16383.0
        scale = jnp.where(smaller, scale * 0.5, scale)
        inverse = jnp.where(smaller, inverse * 2.0, inverse)
        exponent = jnp.where(smaller, exponent + 1.0, exponent)
    spread = jnp.broadcast_to(inverse, (HALF, BRANCH)).T
    q = jnp.round(x * jnp.concatenate([spread, spread], axis=1))
    high = jnp.floor(q * (1.0 / 256.0))
    q_hi[...] = high.astype(BF16)
    q_lo[...] = (q - high * 256.0).astype(BF16)

    def told(rank, number):
        line = iota((HALF, BRANCH), 0)
        words = jnp.where(line == rank, (number >> 5).astype(F32), 0.0)
        words = words + jnp.where(line == rank + 16, (number & 31).astype(F32), 0.0)
        return (words + jnp.where(line == rank + 32, exponent, 0.0)).astype(BF16)

    s_own, s_off = sowner[...], soffset[...]
    s_from, s_to = s_own[0:1, :], s_own[1:2, :]
    hot_0, hot_1, s_0, s_1 = ranks_of(s_from, s_to)

    def asked(rank, offset):
        line = iota((HALF, offset.shape[1]), 0)
        return jnp.where(line == rank + 48, offset.astype(F32), 0.0).astype(BF16)

    slots = slot[...]
    words = nt(hot_from, told(r_from, slots[0:1, :])) + nt(hot_to, told(r_to, slots[1:2, :]))
    words = words + nt(hot_0, asked(s_0, s_off[0:1, :])) + nt(hot_1, asked(s_1, s_off[1:2, :]))
    send[:, CAP : CAP + 1, :] = words.astype(I32).reshape(DEV, 1, HALF)

    chunk = 256

    def word_of(value):
        return (value[:, :HALF] << 16) | (value[:, HALF:] & 0xFFFF)

    def fill(t, _):
        place = iota((chunk, BRANCH), 0) + t * chunk
        sign = (place == p_to).astype(F32) - (place == p_from).astype(F32)
        sign = sign.astype(BF16)
        value = (nn(sign, q_hi[...]) * 256.0 + nn(sign, q_lo[...])).astype(I32)
        word = word_of(value).reshape(chunk // CAP, CAP, HALF)
        send[pl.ds(t * (chunk // CAP), chunk // CAP), 0:CAP, :] = word
        return 0

    pl.semaphore_wait(barrier, ROWS - 1 + COLS - 1)

    def pass_on(t, _):
        there = (lax.rem(row + t, ROWS), col)
        pl.semaphore_signal(ready, inc=1, device_id=there, device_id_type=MESH)
        return 0

    lax.fori_loop(1, ROWS, pass_on, 0)
    lax.fori_loop(0, SLOTS // chunk, fill, 0)
    pl.semaphore_wait(ready, ROWS - 1)

    def out(t, _):
        other = lax.rem(me + t * STRIDE, DEV)
        pltpu.make_async_remote_copy(
            send.at[other], recv.at[me], v_send, v_recv,
            device_id=device_of(other), device_id_type=MESH,
        ).start()
        return 0

    lax.fori_loop(1, DEV, out, 0)
    self_v = pltpu.make_async_copy(send.at[me], recv.at[me], self_sem.at[0])
    self_v.start()
    span = 2 * SCAP
    asks = DEV * span

    acc[...] = jnp.zeros_like(acc)

    def landed(step, _):
        for copy in fetch(step):
            copy.wait()
        return 0

    lax.fori_loop(0, steps, landed, 0)

    def delayed(step, _):
        for i in range(2):
            total = acc[pl.ds(i * BLK, BLK), :]
            for k in range(2):
                d = delays[i, step * 2 + k]
                at = pl.ds(pl.multiple_of(step * width + k * BLK, BLK), BLK)
                source = held[jnp.maximum(d - 1, 0), at, :]
                part = nn(coef[step, pl.ds(i * BLK, BLK), pl.ds(k * BLK, BLK)], source)
                total = total + jnp.where(d > 0, part, 0.0)
            acc[pl.ds(i * BLK, BLK), :] = total
        return 0

    lax.fori_loop(0, steps, delayed, 0)

    self_v.wait()
    rest = pl.ds(0, DEV - 1)
    pltpu.make_async_copy(recv.at[rest], recv.at[rest], v_recv).wait()
    heard = recv[:, CAP : CAP + 1, :].reshape(DEV, HALF).astype(F32).astype(BF16)
    expand = ((iota((DEV, SLOTS), 1) >> 4) == iota((DEV, SLOTS), 0)).astype(BF16)
    wide = tn(heard, expand)
    line = iota((16, SLOTS), 0)
    mine = line == (iota((16, SLOTS), 1) & 15)

    def picked(first):
        return jnp.sum(jnp.where(mine, wide[first : first + 16, :], 0.0), axis=0, keepdims=True)

    node = (picked(0) * 32.0 + picked(16)).astype(I32)
    weight = picked(32).astype(I32)
    weight = jnp.where(weight > 0, power(weight - 1, -1) * 2.0**-12, 0.0)

    share = acc.shape[0] // COLS
    def unpack(t, _):
        at = pl.ds(pl.multiple_of(t * chunk, chunk), chunk)
        w = recv[pl.ds(t * (chunk // CAP), chunk // CAP), 0:CAP, :].reshape(chunk, HALF)
        planes[at, 0 * HALF : 1 * HALF] = (w >> 24).astype(F32).astype(BF16)
        planes[at, 1 * HALF : 2 * HALF] = ((w << 16) >> 24).astype(F32).astype(BF16)
        planes[at, 2 * HALF : 3 * HALF] = ((w >> 16) & 255).astype(F32).astype(BF16)
        planes[at, 3 * HALF : 4 * HALF] = (w & 255).astype(F32).astype(BF16)
        return 0

    lax.fori_loop(0, SLOTS // chunk, unpack, 0)
    past_copy.wait()

    xpos, core = row // CORES, lax.rem(row, CORES)
    right, left, far = lax.rem(xpos + 1, XS), lax.rem(xpos + XS - 1, XS), lax.rem(xpos + 2, XS)
    other = 1 - core

    def piece(at_x, at_core, j):
        start = (at_x * CORES + at_core) * OWN + j * PIECE
        return pl.ds(pl.multiple_of(start, PIECE), PIECE)

    def move(at_x, at_core, j, to_x, to_core, sem, recv_sem):
        at = piece(at_x, at_core, j)
        return pltpu.make_async_remote_copy(
            gathered.at[at], gathered.at[at], sem, recv_sem,
            device_id=(to_x * CORES + to_core, col), device_id_type=MESH,
        )

    def arrived(at_x, at_core, j, recv_sem):
        at = piece(at_x, at_core, j)
        pltpu.make_async_copy(gathered.at[at], gathered.at[at], recv_sem).wait()

    def write(at_x, at_core, j):
        at = piece(at_x, at_core, j)
        return pltpu.make_async_copy(gathered.at[at], charge_out.at[at], w_sem.at[at_x * CORES + at_core, j])

    def use(at_x, at_core, j):
        block = (at_x * CORES + at_core) * PIECES + j
        write(at_x, at_core, j).start()
        source = gathered[piece(at_x, at_core, j), :]
        at = pl.ds(pl.multiple_of(lax.rem(j, 2) * BLK, BLK), BLK)
        for i in range(2):
            part = nn(coef[block // 2, pl.ds(i * BLK, BLK), at], source)
            acc[pl.ds(i * BLK, BLK), :] += jnp.where(delays[i, block] == 0, part, 0.0)

    def turn(t):
        return lax.rem(t, 2) * 2 + t // 2

    def settle(t, _):
        j = turn(t)
        spot = iota((PIECE, SLOTS), 0) + j * PIECE
        gate = jnp.where(spot == node, weight, 0.0).astype(BF16)
        both = nn(gate, planes[...])
        rise = both[:, :EXC] * 256.0 + both[:, EXC:]
        fresh = past[pl.ds(pl.multiple_of(j * PIECE, PIECE), PIECE), :].astype(F32) + rise
        gathered[piece(xpos, core, j), :] = fresh.astype(BF16)
        move(xpos, core, j, right, core, g_send.at[0, j], g_near.at[0, j]).start()
        move(xpos, core, j, left, core, g_send.at[1, j], g_near.at[1, j]).start()
        move(xpos, core, j, xpos, other, g_send.at[2, j], g_pair.at[0, j]).start()
        return 0

    lax.fori_loop(0, PIECES, settle, 0)

    expand = ((iota((DEV, asks), 1) >> 3) == iota((DEV, asks), 0)).astype(BF16)
    wide = tn(heard, expand)[48:56, :]
    line = iota((span, asks), 0)
    mine = line == (iota((span, asks), 1) & (span - 1))
    place = jnp.sum(jnp.where(mine, wide, 0.0), axis=0, keepdims=True).astype(I32)
    take[...] = (iota((share, asks), 0) == place).astype(BF16)

    def near(t, _):
        j = turn(t)
        arrived(left, core, j, g_near.at[0, j])

        @pl.when(j < 2)
        def _():
            move(left, core, j, right, core, g_send.at[3, j], g_near.at[2, j]).start()

        move(left, core, j, xpos, other, g_send.at[4, j], g_pair.at[1, j]).start()
        use(xpos, core, j)
        arrived(right, core, j, g_near.at[1, j])

        @pl.when(j >= 2)
        def _():
            move(right, core, j, left, core, g_send.at[3, j], g_near.at[2, j]).start()

        move(right, core, j, xpos, other, g_send.at[5, j], g_pair.at[2, j]).start()
        use(left, core, j)
        use(right, core, j)
        arrived(xpos, other, j, g_pair.at[0, j])
        use(xpos, other, j)
        return 0

    lax.fori_loop(0, PIECES, near, 0)

    def distant(t, _):
        j = turn(t)
        arrived(far, core, j, g_near.at[2, j])
        move(far, core, j, xpos, other, g_send.at[6, j], g_pair.at[3, j]).start()
        arrived(left, other, j, g_pair.at[1, j])
        use(left, other, j)
        arrived(right, other, j, g_pair.at[2, j])
        use(right, other, j)
        use(far, core, j)
        return 0

    lax.fori_loop(0, PIECES, distant, 0)

    def last(t, _):
        j = turn(t)
        arrived(far, other, j, g_pair.at[3, j])
        use(far, other, j)
        return 0

    lax.fori_loop(0, PIECES, last, 0)

    def give(t, _):
        to = lax.rem(col + t, COLS)
        value = acc[pl.ds(pl.multiple_of(to * share, share), share), :]
        top = jnp.max(jnp.abs(value), axis=0, keepdims=True)
        up, number = coded(value, top)
        p_send[to, 0:share, :] = word_of(number.astype(I32))
        p_send[to, share : share + 1, :] = up[:, :HALF]
        p_send[to, share + 1 : share + 2, :] = up[:, HALF:]

        @pl.when(t < COLS)
        def _():
            pltpu.make_async_remote_copy(
                p_send.at[to], p_recv.at[col], r_send, r_recv,
                device_id=(row, to), device_id_type=MESH,
            ).start()

        return 0

    lax.fori_loop(1, COLS + 1, give, 0)
    self_p = pltpu.make_async_copy(p_send.at[col], p_recv.at[col], self_sem.at[1])
    self_p.start()
    self_p.wait()
    rest = pl.ds(0, COLS - 1)
    pltpu.make_async_copy(p_recv.at[rest], p_recv.at[rest], r_recv).wait()

    def gain(n, totals):
        w = p_recv[n, 0:share, :]
        factor = power(p_recv[n, share : share + 2, :], 1) * LEAST
        a = totals[0] + (w >> 16).astype(F32) * factor[0:1, :]
        b = totals[1] + ((w << 16) >> 16).astype(F32) * factor[1:2, :]
        return a, b

    zero = jnp.zeros((share, HALF), F32)
    a, b = lax.fori_loop(0, COLS, gain, (zero, zero))

    top = jnp.max(jnp.maximum(jnp.abs(a), jnp.abs(b)), axis=0, keepdims=True)
    up, number_a = coded(a, top)
    number = jnp.concatenate([number_a, coded(b, top)[1]], axis=1)
    answer[:, SCAP : SCAP + 1, :] = jnp.broadcast_to(up.reshape(1, 1, HALF), (DEV, 1, HALF))
    high = jnp.floor(number * (1.0 / 256.0))
    low = (number - high * 256.0).astype(BF16)
    high = high.astype(BF16)

    def reply(t, _):
        g = lax.rem(row + t, ROWS)
        chosen = take[:, pl.ds(pl.multiple_of(g * HALF, HALF), HALF)]
        value = (tn(chosen, high) * 256.0 + tn(chosen, low)).astype(I32)
        word = word_of(value).reshape(COLS, span, HALF)
        answer[pl.ds(g * COLS, COLS), 0:SCAP, :] = word[:, :SCAP, :]

        def send_answer(n, _):
            to = g * COLS + lax.rem(col + n, COLS)

            @pl.when(to != me)
            def _():
                pltpu.make_async_remote_copy(
                    answer.at[to], replies.at[me], a_send, a_recv,
                    device_id=device_of(to), device_id_type=MESH,
                ).start()

            return 0

        lax.fori_loop(0, COLS, send_answer, 0)
        return 0

    lax.fori_loop(0, asks // HALF, reply, 0)
    self_a = pltpu.make_async_copy(answer.at[me], replies.at[me], self_sem.at[2])
    self_a.start()

    for n in range(7):
        def left_here(j, _):
            at = piece(xpos, core, j)
            pltpu.make_async_copy(gathered.at[at], gathered.at[at], g_send.at[n, j]).wait()
            return 0

        lax.fori_loop(0, PIECES, left_here, 0)

    def written(n, _):
        write(n // CORES // PIECES, lax.rem(n // PIECES, CORES), lax.rem(n, PIECES)).wait()
        return 0

    lax.fori_loop(0, ROWS * PIECES, written, 0)
    rest = pl.ds(0, DEV - 1)
    pltpu.make_async_copy(send.at[rest], send.at[rest], v_send).wait()
    rest = pl.ds(0, COLS - 1)
    pltpu.make_async_copy(p_send.at[rest], p_send.at[rest], r_send).wait()
    self_a.wait()
    rest = pl.ds(0, DEV - 1)
    pltpu.make_async_copy(replies.at[rest], replies.at[rest], a_recv).wait()
    pltpu.make_async_copy(answer.at[rest], answer.at[rest], a_send).wait()


def emit_kernel(
    charge, replies_h, sowner_h, charge_now, drops, block, replies, sowner, in_sem, out_sem, small_sem
):
    span = charge.shape[0] // 8

    def load(part):
        at = pl.ds(part * span, span)
        return pltpu.make_async_copy(charge.at[at], block.at[at], in_sem.at[part])

    def save(part):
        at = pl.ds(part * span, span)
        return pltpu.make_async_copy(block.at[at], charge_now.at[at], out_sem.at[part])

    few = pltpu.make_async_copy(sowner_h, sowner, small_sem.at[0])
    told = pltpu.make_async_copy(replies_h, replies, small_sem.at[1])
    few.start()
    for part in range(8):
        load(part).start()
    told.start()
    few.wait()
    s_own = sowner[...]
    s_from, s_to = s_own[0:1, :], s_own[1:2, :]
    _, _, s_0, s_1 = ranks_of(s_from, s_to)
    wide = 2 * SCAP
    asks = DEV * wide
    line = iota((asks, s_own.shape[1]), 0)
    gate = (line == s_from * wide + s_0).astype(F32) - (line == s_to * wide + s_1).astype(F32)
    gate = gate.astype(BF16)
    for part in range(8):
        load(part).wait()
        save(part).start()
    told.wait()
    w = replies[:, 0:SCAP, :]
    up = replies[:, SCAP : SCAP + 1, :].reshape(DEV, HALF)
    factor = (power(up, 1) * LEAST).reshape(DEV, 1, HALF)
    for half in range(2):
        number = (w >> 16) if half == 0 else ((w << 16) >> 16)
        value = number.astype(F32) * factor
        value = jnp.concatenate([value, value], axis=1).reshape(asks, HALF)
        high, low = split(value)
        drops[:, half * HALF : (half + 1) * HALF] = tn(gate, high) + tn(gate, low)
    for part in range(8):
        save(part).wait()


def emit(charge, replies, sowner):
    vmem, hbm = pl.BlockSpec(memory_space=pltpu.VMEM), pl.BlockSpec(memory_space=pl.ANY)
    dma = pltpu.SemaphoreType.DMA
    return pl.pallas_call(
        emit_kernel,
        out_shape=(
            jax.ShapeDtypeStruct(charge.shape, BF16),
            jax.ShapeDtypeStruct((sowner.shape[1], EXC), F32),
        ),
        in_specs=[hbm, hbm, hbm],
        out_specs=(hbm, vmem),
        scratch_shapes=[
            pltpu.VMEM(charge.shape, BF16),
            pltpu.VMEM(replies.shape, I32),
            pltpu.VMEM(sowner.shape, I32),
            dma((8,)), dma((8,)), dma((2,)),
        ],
        compiler_params=pltpu.CompilerParams(vmem_limit_bytes=FULL),
        name="emit",
    )(charge, replies, sowner)


def split(value):
    top = value.astype(BF16)
    return top, (value - top.astype(F32)).astype(BF16)


def step(cur, owner, slot, sowner, soffset, hist, coef, delays):
    hbm = pl.BlockSpec(memory_space=pl.ANY)
    nodes, rows = hist.shape[1], coef.shape[0]
    width = 2 * BLK
    dma = pltpu.SemaphoreType.DMA
    asks = DEV * 2 * SCAP
    return pl.pallas_call(
        step_kernel,
        out_shape=(
            jax.ShapeDtypeStruct((nodes, EXC), BF16),
            jax.ShapeDtypeStruct((DEV, SCAP + 1, HALF), I32),
        ),
        in_specs=[hbm] * 8,
        out_specs=(hbm, hbm),
        scratch_shapes=[
            pltpu.VMEM(cur.shape, F32),
            pltpu.VMEM(owner.shape, I32),
            pltpu.VMEM(slot.shape, I32),
            pltpu.VMEM(sowner.shape, I32),
            pltpu.VMEM(soffset.shape, I32),
            pltpu.SMEM(delays.shape, I32),
            pltpu.VMEM((DEV, CAP + 1, HALF), I32),
            pltpu.VMEM((DEV, CAP + 1, HALF), I32),
            pltpu.VMEM((SLOTS, 2 * EXC), BF16),
            pltpu.VMEM((BRANCH, EXC), BF16),
            pltpu.VMEM((BRANCH, EXC), BF16),
            pltpu.VMEM((OWN, EXC), BF16),
            pltpu.VMEM((nodes // width, rows, width), BF16),
            pltpu.VMEM(hist.shape, BF16),
            pltpu.VMEM((rows, EXC), F32),
            pltpu.VMEM((nodes, EXC), BF16),
            pltpu.VMEM((rows // COLS, asks), BF16),
            pltpu.VMEM((COLS, rows // COLS + 2, HALF), I32),
            pltpu.VMEM((COLS, rows // COLS + 2, HALF), I32),
            pltpu.VMEM((DEV, SCAP + 1, HALF), I32),
            dma((6,)), dma, dma, dma((3,)), dma, dma, dma((nodes // width,)), dma((ROWS, PIECES)),
            dma((7, PIECES)), dma((3, PIECES)), dma((4, PIECES)),
            dma, dma, dma, dma, pltpu.SemaphoreType.REGULAR,
        ],
        compiler_params=pltpu.CompilerParams(
            collective_id=0, has_side_effects=True, vmem_limit_bytes=FULL
        ),
        name="step",
    )(cur, owner, slot, sowner, soffset, hist, coef, delays)


def local(
    currents, branch_owner, branch_slot, history, coefficients, delays, slab_owner, slab_offset
):
    sowner = slab_owner.T
    charge, replies = step(
        currents, branch_owner.T, branch_slot.T, sowner, slab_offset.T, history, coefficients, delays
    )
    return emit(charge, replies, sowner)


def solution(mesh):
    placed = (
        P(("row", "col"), None),
        P(("row", "col"), None),
        P(("row", "col"), None),
        P(None, "col", None),
        P("row", "col"),
        P("row", "col"),
        P(("row", "col"), None),
        P(("row", "col"), None),
    )
    return jax.shard_map(
        local,
        mesh=mesh,
        in_specs=placed,
        out_specs=(P("col", None), P(("row", "col"), None)),
        check_vma=False,
    )
```

```python
import functools

import jax
import jax.numpy as jnp
from jax import lax
from jax.experimental import pallas as pl
from jax.experimental.pallas import tpu as pltpu
from jax.sharding import PartitionSpec as P

F32 = jnp.float32
BF16 = jnp.bfloat16
I32 = jnp.int32
MESH = pl.DeviceIdType.MESH

ROWS = 8
COLS = 16
DEV = ROWS * COLS
CORES = 2
XS = ROWS // CORES
BRANCH = 256
CAP = 16
SCAP = 4
OWN = 1024
EXC = 256
HALF = 128
SLOTS = DEV * CAP
BLK = 256
PIECES = 4
PIECE = OWN // PIECES
FULL = 67043328
STRIDE = 1
LEAST = 2.0**-80


def iota(shape, dim):
    return lax.broadcasted_iota(I32, shape, dim)


def nn(a, b):
    return lax.dot_general(a, b, (((1,), (0,)), ((), ())), preferred_element_type=F32)


def nt(a, b):
    return lax.dot_general(a, b, (((1,), (1,)), ((), ())), preferred_element_type=F32)


def tn(a, b):
    return lax.dot_general(a, b, (((0,), (0,)), ((), ())), preferred_element_type=F32)


def power(exponent, sign):
    result = jnp.ones(exponent.shape, F32)
    for bit in range(7):
        factor = 2.0 ** (sign * (1 << bit))
        result = result * jnp.where(((exponent >> bit) & 1) > 0, factor, 1.0)
    return result


def coded(value, top):
    up = jnp.zeros(top.shape, I32)
    unit = jnp.full(top.shape, LEAST, F32)
    inverse = jnp.full(top.shape, 1.0 / LEAST, F32)
    for bit in (6, 5, 4, 3, 2, 1, 0):
        leap = 1 << bit
        larger = top > unit * (32766.0 * 2.0 ** (leap - 1))
        up = jnp.where(larger, up + leap, up)
        unit = jnp.where(larger, unit * 2.0**leap, unit)
        inverse = jnp.where(larger, inverse * 2.0**-leap, inverse)
    return up, jnp.round(value * inverse)


def device_of(index):
    return (index // COLS, lax.rem(index, COLS))


def ranks_of(first, second):
    n = first.shape[1]
    hot_a = iota((DEV, n), 0) == first
    hot_b = iota((DEV, n), 0) == second
    a, b = hot_a.astype(F32), hot_b.astype(F32)
    before = (iota((n, n), 0) < iota((n, n), 1)).astype(BF16)
    seen_a = nn(a.astype(BF16), before)
    seen_b = nn(b.astype(BF16), before) + jnp.sum(a, axis=1, keepdims=True)
    rank_a = jnp.sum(a * seen_a, axis=0, keepdims=True).astype(I32)
    rank_b = jnp.sum(b * seen_b, axis=0, keepdims=True).astype(I32)
    return a.astype(BF16), b.astype(BF16), rank_a, rank_b


def greet(row, col):
    barrier = pltpu.get_barrier_semaphore()

    def down(t, _):
        there = (lax.rem(row + t, ROWS), col)
        pl.semaphore_signal(barrier, inc=1, device_id=there, device_id_type=MESH)
        return 0

    def along(t, _):
        there = (row, lax.rem(col + t, COLS))
        pl.semaphore_signal(barrier, inc=1, device_id=there, device_id_type=MESH)
        return 0

    lax.fori_loop(1, ROWS, down, 0)
    lax.fori_loop(1, COLS, along, 0)
    return barrier


def step_kernel(
    cur_h, owner_h, slot_h, sowner_h, soffset_h, hist, coef_h, delays_h,
    charge_out, replies,
    cur, owner, slot, sowner, soffset, delays,
    send, recv, planes, q_hi, q_lo, past, coef, held, acc, gathered,
    take, p_send, p_recv, answer,
    first_sem, v_send, v_recv, self_sem, past_sem, h_sem, c_sem, w_sem,
    g_send, g_near, g_pair, r_send, r_recv, a_send, a_recv, ready,
):
    row, col = lax.axis_index("row"), lax.axis_index("col")
    me = row * COLS + col
    barrier = greet(row, col)
    small = ((cur_h, cur), (owner_h, owner), (slot_h, slot), (sowner_h, sowner), (soffset_h, soffset), (delays_h, delays))
    small = [pltpu.make_async_copy(a, b, first_sem.at[n]) for n, (a, b) in enumerate(small)]
    for copy in small:
        copy.start()
    past_copy = pltpu.make_async_copy(hist.at[0, pl.ds(pl.multiple_of(row * OWN, OWN), OWN)], past, past_sem)
    past_copy.start()

    width = 2 * BLK
    steps = coef.shape[0]

    def fetch(step):
        at = pl.ds(pl.multiple_of(step * width, width), width)
        return (
            pltpu.make_async_copy(hist.at[:, at], held.at[:, at], h_sem),
            pltpu.make_async_copy(coef_h.at[:, at], coef.at[step], c_sem.at[step]),
        )

    def bring(step, _):
        for copy in fetch(step):
            copy.start()
        return 0

    lax.fori_loop(0, steps, bring, 0)
    for copy in small:
        copy.wait()

    own = owner[...]
    targets = (own & (ROWS - 1)) * COLS + (own >> 3)
    t_from, t_to = targets[0:1, :], targets[1:2, :]
    hot_from, hot_to, r_from, r_to = ranks_of(t_from, t_to)
    p_from, p_to = t_from * CAP + r_from, t_to * CAP + r_to
    x = cur[...]
    size = jnp.abs(x)
    size = jnp.maximum(size[:, :HALF], size[:, HALF:])
    largest = jnp.max(size.T, axis=0, keepdims=True)
    scale = jnp.full((1, BRANCH), 2.0**-12, F32)
    inverse = jnp.full((1, BRANCH), 2.0**12, F32)
    exponent = jnp.ones((1, BRANCH), F32)
    for _ in range(32):
        smaller = largest <= scale * 16383.0
        scale = jnp.where(smaller, scale * 0.5, scale)
        inverse = jnp.where(smaller, inverse * 2.0, inverse)
        exponent = jnp.where(smaller, exponent + 1.0, exponent)
    spread = jnp.broadcast_to(inverse, (HALF, BRANCH)).T
    q = jnp.round(x * jnp.concatenate([spread, spread], axis=1))
    high = jnp.floor(q * (1.0 / 256.0))
    q_hi[...] = high.astype(BF16)
    q_lo[...] = (q - high * 256.0).astype(BF16)

    def told(rank, number):
        line = iota((HALF, BRANCH), 0)
        words = jnp.where(line == rank, (number >> 5).astype(F32), 0.0)
        words = words + jnp.where(line == rank + 16, (number & 31).astype(F32), 0.0)
        return (words + jnp.where(line == rank + 32, exponent, 0.0)).astype(BF16)

    s_own, s_off = sowner[...], soffset[...]
    s_from, s_to = s_own[0:1, :], s_own[1:2, :]
    hot_0, hot_1, s_0, s_1 = ranks_of(s_from, s_to)

    def asked(rank, offset):
        line = iota((HALF, offset.shape[1]), 0)
        return jnp.where(line == rank + 48, offset.astype(F32), 0.0).astype(BF16)

    slots = slot[...]
    words = nt(hot_from, told(r_from, slots[0:1, :])) + nt(hot_to, told(r_to, slots[1:2, :]))
    words = words + nt(hot_0, asked(s_0, s_off[0:1, :])) + nt(hot_1, asked(s_1, s_off[1:2, :]))
    send[:, CAP : CAP + 1, :] = words.astype(I32).reshape(DEV, 1, HALF)

    chunk = 256

    def word_of(value):
        return (value[:, :HALF] << 16) | (value[:, HALF:] & 0xFFFF)

    def fill(t, _):
        place = iota((chunk, BRANCH), 0) + t * chunk
        sign = (place == p_to).astype(F32) - (place == p_from).astype(F32)
        sign = sign.astype(BF16)
        value = (nn(sign, q_hi[...]) * 256.0 + nn(sign, q_lo[...])).astype(I32)
        word = word_of(value).reshape(chunk // CAP, CAP, HALF)
        send[pl.ds(t * (chunk // CAP), chunk // CAP), 0:CAP, :] = word
        return 0

    pl.semaphore_wait(barrier, ROWS - 1 + COLS - 1)

    def pass_on(t, _):
        there = (lax.rem(row + t, ROWS), col)
        pl.semaphore_signal(ready, inc=1, device_id=there, device_id_type=MESH)
        return 0

    lax.fori_loop(1, ROWS, pass_on, 0)
    lax.fori_loop(0, SLOTS // chunk, fill, 0)
    pl.semaphore_wait(ready, ROWS - 1)

    def out(t, _):
        other = lax.rem(me + t * STRIDE, DEV)
        pltpu.make_async_remote_copy(
            send.at[other], recv.at[me], v_send, v_recv,
            device_id=device_of(other), device_id_type=MESH,
        ).start()
        return 0

    lax.fori_loop(1, DEV, out, 0)
    self_v = pltpu.make_async_copy(send.at[me], recv.at[me], self_sem.at[0])
    self_v.start()
    span = 2 * SCAP
    asks = DEV * span

    acc[...] = jnp.zeros_like(acc)

    def landed(step, _):
        for copy in fetch(step):
            copy.wait()
        return 0

    lax.fori_loop(0, steps, landed, 0)

    def delayed(step, _):
        for i in range(2):
            total = acc[pl.ds(i * BLK, BLK), :]
            for k in range(2):
                d = delays[i, step * 2 + k]
                at = pl.ds(pl.multiple_of(step * width + k * BLK, BLK), BLK)
                source = held[jnp.maximum(d - 1, 0), at, :]
                part = nn(coef[step, pl.ds(i * BLK, BLK), pl.ds(k * BLK, BLK)], source)
                total = total + jnp.where(d > 0, part, 0.0)
            acc[pl.ds(i * BLK, BLK), :] = total
        return 0

    lax.fori_loop(0, steps, delayed, 0)

    self_v.wait()
    rest = pl.ds(0, DEV - 1)
    pltpu.make_async_copy(recv.at[rest], recv.at[rest], v_recv).wait()
    heard = recv[:, CAP : CAP + 1, :].reshape(DEV, HALF).astype(F32).astype(BF16)
    expand = ((iota((DEV, SLOTS), 1) >> 4) == iota((DEV, SLOTS), 0)).astype(BF16)
    wide = tn(heard, expand)
    line = iota((16, SLOTS), 0)
    mine = line == (iota((16, SLOTS), 1) & 15)

    def picked(first):
        return jnp.sum(jnp.where(mine, wide[first : first + 16, :], 0.0), axis=0, keepdims=True)

    node = (picked(0) * 32.0 + picked(16)).astype(I32)
    weight = picked(32).astype(I32)
    weight = jnp.where(weight > 0, power(weight - 1, -1) * 2.0**-12, 0.0)

    share = acc.shape[0] // COLS
    def unpack(t, _):
        at = pl.ds(pl.multiple_of(t * chunk, chunk), chunk)
        w = recv[pl.ds(t * (chunk // CAP), chunk // CAP), 0:CAP, :].reshape(chunk, HALF)
        planes[at, 0 * HALF : 1 * HALF] = (w >> 24).astype(F32).astype(BF16)
        planes[at, 1 * HALF : 2 * HALF] = ((w << 16) >> 24).astype(F32).astype(BF16)
        planes[at, 2 * HALF : 3 * HALF] = ((w >> 16) & 255).astype(F32).astype(BF16)
        planes[at, 3 * HALF : 4 * HALF] = (w & 255).astype(F32).astype(BF16)
        return 0

    lax.fori_loop(0, SLOTS // chunk, unpack, 0)
    past_copy.wait()

    xpos, core = row // CORES, lax.rem(row, CORES)
    right, left, far = lax.rem(xpos + 1, XS), lax.rem(xpos + XS - 1, XS), lax.rem(xpos + 2, XS)
    other = 1 - core

    def piece(at_x, at_core, j):
        start = (at_x * CORES + at_core) * OWN + j * PIECE
        return pl.ds(pl.multiple_of(start, PIECE), PIECE)

    def move(at_x, at_core, j, to_x, to_core, sem, recv_sem):
        at = piece(at_x, at_core, j)
        return pltpu.make_async_remote_copy(
            gathered.at[at], gathered.at[at], sem, recv_sem,
            device_id=(to_x * CORES + to_core, col), device_id_type=MESH,
        )

    def arrived(at_x, at_core, j, recv_sem):
        at = piece(at_x, at_core, j)
        pltpu.make_async_copy(gathered.at[at], gathered.at[at], recv_sem).wait()

    def write(at_x, at_core, j):
        at = piece(at_x, at_core, j)
        return pltpu.make_async_copy(gathered.at[at], charge_out.at[at], w_sem.at[at_x * CORES + at_core, j])

    def use(at_x, at_core, j):
        block = (at_x * CORES + at_core) * PIECES + j
        write(at_x, at_core, j).start()
        source = gathered[piece(at_x, at_core, j), :]
        at = pl.ds(pl.multiple_of(lax.rem(j, 2) * BLK, BLK), BLK)
        for i in range(2):
            part = nn(coef[block // 2, pl.ds(i * BLK, BLK), at], source)
            acc[pl.ds(i * BLK, BLK), :] += jnp.where(delays[i, block] == 0, part, 0.0)

    def turn(t):
        return lax.rem(t, 2) * 2 + t // 2

    def settle(t, _):
        j = turn(t)
        spot = iota((PIECE, SLOTS), 0) + j * PIECE
        gate = jnp.where(spot == node, weight, 0.0).astype(BF16)
        both = nn(gate, planes[...])
        rise = both[:, :EXC] * 256.0 + both[:, EXC:]
        fresh = past[pl.ds(pl.multiple_of(j * PIECE, PIECE), PIECE), :].astype(F32) + rise
        gathered[piece(xpos, core, j), :] = fresh.astype(BF16)
        move(xpos, core, j, right, core, g_send.at[0, j], g_near.at[0, j]).start()
        move(xpos, core, j, left, core, g_send.at[1, j], g_near.at[1, j]).start()
        move(xpos, core, j, xpos, other, g_send.at[2, j], g_pair.at[0, j]).start()
        return 0

    lax.fori_loop(0, PIECES, settle, 0)

    expand = ((iota((DEV, asks), 1) >> 3) == iota((DEV, asks), 0)).astype(BF16)
    wide = tn(heard, expand)[48:56, :]
    line = iota((span, asks), 0)
    mine = line == (iota((span, asks), 1) & (span - 1))
    place = jnp.sum(jnp.where(mine, wide, 0.0), axis=0, keepdims=True).astype(I32)
    take[...] = (iota((share, asks), 0) == place).astype(BF16)

    def near(t, _):
        j = turn(t)
        arrived(left, core, j, g_near.at[0, j])

        @pl.when(j < 2)
        def _():
            move(left, core, j, right, core, g_send.at[3, j], g_near.at[2, j]).start()

        move(left, core, j, xpos, other, g_send.at[4, j], g_pair.at[1, j]).start()
        use(xpos, core, j)
        arrived(right, core, j, g_near.at[1, j])

        @pl.when(j >= 2)
        def _():
            move(right, core, j, left, core, g_send.at[3, j], g_near.at[2, j]).start()

        move(right, core, j, xpos, other, g_send.at[5, j], g_pair.at[2, j]).start()
        use(left, core, j)
        use(right, core, j)
        arrived(xpos, other, j, g_pair.at[0, j])
        use(xpos, other, j)
        return 0

    lax.fori_loop(0, PIECES, near, 0)

    def distant(t, _):
        j = turn(t)
        arrived(far, core, j, g_near.at[2, j])
        move(far, core, j, xpos, other, g_send.at[6, j], g_pair.at[3, j]).start()
        arrived(left, other, j, g_pair.at[1, j])
        use(left, other, j)
        arrived(right, other, j, g_pair.at[2, j])
        use(right, other, j)
        use(far, core, j)
        return 0

    lax.fori_loop(0, PIECES, distant, 0)

    def last(t, _):
        j = turn(t)
        arrived(far, other, j, g_pair.at[3, j])
        use(far, other, j)
        return 0

    lax.fori_loop(0, PIECES, last, 0)

    def give(t, _):
        to = lax.rem(col + t, COLS)
        value = acc[pl.ds(pl.multiple_of(to * share, share), share), :]
        top = jnp.max(jnp.abs(value), axis=0, keepdims=True)
        up, number = coded(value, top)
        p_send[to, 0:share, :] = word_of(number.astype(I32))
        p_send[to, share : share + 1, :] = up[:, :HALF]
        p_send[to, share + 1 : share + 2, :] = up[:, HALF:]

        @pl.when(t < COLS)
        def _():
            pltpu.make_async_remote_copy(
                p_send.at[to], p_recv.at[col], r_send, r_recv,
                device_id=(row, to), device_id_type=MESH,
            ).start()

        return 0

    lax.fori_loop(1, COLS + 1, give, 0)
    self_p = pltpu.make_async_copy(p_send.at[col], p_recv.at[col], self_sem.at[1])
    self_p.start()
    self_p.wait()
    rest = pl.ds(0, COLS - 1)
    pltpu.make_async_copy(p_recv.at[rest], p_recv.at[rest], r_recv).wait()

    def gain(n, totals):
        w = p_recv[n, 0:share, :]
        factor = power(p_recv[n, share : share + 2, :], 1) * LEAST
        a = totals[0] + (w >> 16).astype(F32) * factor[0:1, :]
        b = totals[1] + ((w << 16) >> 16).astype(F32) * factor[1:2, :]
        return a, b

    zero = jnp.zeros((share, HALF), F32)
    a, b = lax.fori_loop(0, COLS, gain, (zero, zero))

    top = jnp.max(jnp.maximum(jnp.abs(a), jnp.abs(b)), axis=0, keepdims=True)
    up, number_a = coded(a, top)
    number = jnp.concatenate([number_a, coded(b, top)[1]], axis=1)
    answer[:, SCAP : SCAP + 1, :] = jnp.broadcast_to(up.reshape(1, 1, HALF), (DEV, 1, HALF))
    high = jnp.floor(number * (1.0 / 256.0))
    low = (number - high * 256.0).astype(BF16)
    high = high.astype(BF16)
    for g in range(asks // HALF):
        chosen = take[:, g * HALF : (g + 1) * HALF]
        value = (tn(chosen, high) * 256.0 + tn(chosen, low)).astype(I32)
        word = word_of(value).reshape(HALF // span, span, HALF)
        answer[pl.ds(g * (HALF // span), HALF // span), 0:SCAP, :] = word[:, :SCAP, :]

    def send_answer(t, _):
        to = lax.rem(me + t * STRIDE, DEV)
        pltpu.make_async_remote_copy(
            answer.at[to], replies.at[me], a_send, a_recv,
            device_id=device_of(to), device_id_type=MESH,
        ).start()
        return 0

    lax.fori_loop(1, DEV, send_answer, 0)
    self_a = pltpu.make_async_copy(answer.at[me], replies.at[me], self_sem.at[2])
    self_a.start()

    for n in range(7):
        def left_here(j, _):
            at = piece(xpos, core, j)
            pltpu.make_async_copy(gathered.at[at], gathered.at[at], g_send.at[n, j]).wait()
            return 0

        lax.fori_loop(0, PIECES, left_here, 0)

    def written(n, _):
        write(n // CORES // PIECES, lax.rem(n // PIECES, CORES), lax.rem(n, PIECES)).wait()
        return 0

    lax.fori_loop(0, ROWS * PIECES, written, 0)
    rest = pl.ds(0, DEV - 1)
    pltpu.make_async_copy(send.at[rest], send.at[rest], v_send).wait()
    rest = pl.ds(0, COLS - 1)
    pltpu.make_async_copy(p_send.at[rest], p_send.at[rest], r_send).wait()
    self_a.wait()
    rest = pl.ds(0, DEV - 1)
    pltpu.make_async_copy(replies.at[rest], replies.at[rest], a_recv).wait()
    pltpu.make_async_copy(answer.at[rest], answer.at[rest], a_send).wait()


def emit_kernel(
    charge, replies_h, sowner_h, charge_now, drops, block, replies, sowner, in_sem, out_sem, small_sem
):
    span = charge.shape[0] // 8

    def load(part):
        at = pl.ds(part * span, span)
        return pltpu.make_async_copy(charge.at[at], block.at[at], in_sem.at[part])

    def save(part):
        at = pl.ds(part * span, span)
        return pltpu.make_async_copy(block.at[at], charge_now.at[at], out_sem.at[part])

    few = pltpu.make_async_copy(sowner_h, sowner, small_sem.at[0])
    told = pltpu.make_async_copy(replies_h, replies, small_sem.at[1])
    few.start()
    for part in range(8):
        load(part).start()
    told.start()
    few.wait()
    s_own = sowner[...]
    s_from, s_to = s_own[0:1, :], s_own[1:2, :]
    _, _, s_0, s_1 = ranks_of(s_from, s_to)
    wide = 2 * SCAP
    asks = DEV * wide
    line = iota((asks, s_own.shape[1]), 0)
    gate = (line == s_from * wide + s_0).astype(F32) - (line == s_to * wide + s_1).astype(F32)
    gate = gate.astype(BF16)
    for part in range(8):
        load(part).wait()
        save(part).start()
    told.wait()
    w = replies[:, 0:SCAP, :]
    up = replies[:, SCAP : SCAP + 1, :].reshape(DEV, HALF)
    factor = (power(up, 1) * LEAST).reshape(DEV, 1, HALF)
    for half in range(2):
        number = (w >> 16) if half == 0 else ((w << 16) >> 16)
        value = number.astype(F32) * factor
        value = jnp.concatenate([value, value], axis=1).reshape(asks, HALF)
        high, low = split(value)
        drops[:, half * HALF : (half + 1) * HALF] = tn(gate, high) + tn(gate, low)
    for part in range(8):
        save(part).wait()


def emit(charge, replies, sowner):
    vmem, hbm = pl.BlockSpec(memory_space=pltpu.VMEM), pl.BlockSpec(memory_space=pl.ANY)
    dma = pltpu.SemaphoreType.DMA
    return pl.pallas_call(
        emit_kernel,
        out_shape=(
            jax.ShapeDtypeStruct(charge.shape, BF16),
            jax.ShapeDtypeStruct((sowner.shape[1], EXC), F32),
        ),
        in_specs=[hbm, hbm, hbm],
        out_specs=(hbm, vmem),
        scratch_shapes=[
            pltpu.VMEM(charge.shape, BF16),
            pltpu.VMEM(replies.shape, I32),
            pltpu.VMEM(sowner.shape, I32),
            dma((8,)), dma((8,)), dma((2,)),
        ],
        compiler_params=pltpu.CompilerParams(vmem_limit_bytes=FULL),
        name="emit",
    )(charge, replies, sowner)


def split(value):
    top = value.astype(BF16)
    return top, (value - top.astype(F32)).astype(BF16)


def step(cur, owner, slot, sowner, soffset, hist, coef, delays):
    hbm = pl.BlockSpec(memory_space=pl.ANY)
    nodes, rows = hist.shape[1], coef.shape[0]
    width = 2 * BLK
    dma = pltpu.SemaphoreType.DMA
    asks = DEV * 2 * SCAP
    return pl.pallas_call(
        step_kernel,
        out_shape=(
            jax.ShapeDtypeStruct((nodes, EXC), BF16),
            jax.ShapeDtypeStruct((DEV, SCAP + 1, HALF), I32),
        ),
        in_specs=[hbm] * 8,
        out_specs=(hbm, hbm),
        scratch_shapes=[
            pltpu.VMEM(cur.shape, F32),
            pltpu.VMEM(owner.shape, I32),
            pltpu.VMEM(slot.shape, I32),
            pltpu.VMEM(sowner.shape, I32),
            pltpu.VMEM(soffset.shape, I32),
            pltpu.SMEM(delays.shape, I32),
            pltpu.VMEM((DEV, CAP + 1, HALF), I32),
            pltpu.VMEM((DEV, CAP + 1, HALF), I32),
            pltpu.VMEM((SLOTS, 2 * EXC), BF16),
            pltpu.VMEM((BRANCH, EXC), BF16),
            pltpu.VMEM((BRANCH, EXC), BF16),
            pltpu.VMEM((OWN, EXC), BF16),
            pltpu.VMEM((nodes // width, rows, width), BF16),
            pltpu.VMEM(hist.shape, BF16),
            pltpu.VMEM((rows, EXC), F32),
            pltpu.VMEM((nodes, EXC), BF16),
            pltpu.VMEM((rows // COLS, asks), BF16),
            pltpu.VMEM((COLS, rows // COLS + 2, HALF), I32),
            pltpu.VMEM((COLS, rows // COLS + 2, HALF), I32),
            pltpu.VMEM((DEV, SCAP + 1, HALF), I32),
            dma((6,)), dma, dma, dma((3,)), dma, dma, dma((nodes // width,)), dma((ROWS, PIECES)),
            dma((7, PIECES)), dma((3, PIECES)), dma((4, PIECES)),
            dma, dma, dma, dma, pltpu.SemaphoreType.REGULAR,
        ],
        compiler_params=pltpu.CompilerParams(
            collective_id=0, has_side_effects=True, vmem_limit_bytes=FULL
        ),
        name="step",
    )(cur, owner, slot, sowner, soffset, hist, coef, delays)


def local(
    currents, branch_owner, branch_slot, history, coefficients, delays, slab_owner, slab_offset
):
    sowner = slab_owner.T
    charge, replies = step(
        currents, branch_owner.T, branch_slot.T, sowner, slab_offset.T, history, coefficients, delays
    )
    return emit(charge, replies, sowner)


def solution(mesh):
    placed = (
        P(("row", "col"), None),
        P(("row", "col"), None),
        P(("row", "col"), None),
        P(None, "col", None),
        P("row", "col"),
        P("row", "col"),
        P(("row", "col"), None),
        P(("row", "col"), None),
    )
    return jax.shard_map(
        local,
        mesh=mesh,
        in_specs=placed,
        out_specs=(P("col", None), P(("row", "col"), None)),
        check_vma=False,
    )
```
